32 devices in a mesh: brick: 16 (over z, y, core), chan: 2 (over x).
Axes of the slice: x: 2, y: 2, z: 4, core: 2. Of those that a mesh axis runs over, the one named last changes fastest.
Arguments:
- features: bfloat16 [512, 8192], P('chan', 'brick'), may hold values from -6 to 6
- positions: float32 [3, 8192], P(None, 'brick'), may hold values from 0 to 1, as said below
- lists: int32 [64, 4], P('brick'), may hold values from 0 to 7, as said below
- counts: int32 [64], P('brick'), may hold values from 1 to 4, as said below
- fourier_filter: float32 [512, 4096], P('chan'), may hold values from 0.5 to 4
- radial_weights: float32 [8, 512], P(None, 'chan'), may hold values from -4 to 4
- norm_gain: float32 [512], replicated, may hold values from 0.1 to 1.9
- mlp_in: bfloat16 [1024, 512], P(None, 'chan'), may hold values from -0.25 to 0.25
- mlp_out: bfloat16 [512, 1024], P('chan'), may hold values from -0.1875 to 0.1875
Outputs:
- updated: bfloat16 [512, 8192], P(None, ('brick', 'chan'))
The draws below stay inside these ranges and needn't reach their ends.
Inputs may be any that keep to these rules, and one draw needn't show every extreme that they name: Row g of lists holds 4 different values from (g mod 4) to (g mod 4) + 4. `counts`: the value 4 occurs in every draw. `positions`: for an atom of block j of its brick (j = its index // 128 mod 4) the first coordinate lies between j / 4 and (j + 1) / 4; the other two lie in [0, 1).
All inputs are finite; a program needn't handle non-finite values.
Results may differ from the reference program's by a relative error of at most 0.0055.
The reference program's roundings to bfloat16 on the way count: a program that leaves them out, or rounds other values in their place, can miss the bound.
Values may be sent and summed in bfloat16 or wider, within the bound.
No kernel may reach another device: no remote copies, remote signals or barrier semaphores. Data moves between devices by JAX's collectives and lax.ppermute only.
A program may use at most 64 MiB of HBM per device.

```python
import math
import jax
import jax.numpy as jnp
from jax import lax

C = 512
KSIDE = 16
NK = 4096
HID = 1024
NBASIS = 8
BLOCK = 128
BLK_DEV = 4
REACH = 2
LIST = 4
A_DEV = 512
ATOMS = 8192
NBLOCKS = 64
N_BRICK = 16


def draw_positions(key, part):
    first_key = jax.random.fold_in(key, 31)
    second_key = jax.random.fold_in(key, 32)
    fraction = jax.random.uniform(first_key, (ATOMS,), jnp.float32, 0.0, 0.999)
    block_local = (jnp.arange(ATOMS, dtype=jnp.int32) // BLOCK % BLK_DEV).astype(jnp.float32)
    along_first = (block_local + fraction) / BLK_DEV
    across = jax.random.uniform(second_key, (2, ATOMS), jnp.float32, 0.0, 0.999)
    return jnp.concatenate([along_first[None, :], across], axis=0)


def draw_lists(key, part):
    window = 2 * REACH + 1
    scores = jax.random.randint(jax.random.fold_in(key, 11), (NBLOCKS, window), 0, 1 << 20) * window
    scores = scores + jnp.arange(window, dtype=jnp.int32)[None, :]
    ordering = jnp.argsort(scores, axis=1, stable=True).astype(jnp.int32)
    local_block = (jnp.arange(NBLOCKS, dtype=jnp.int32) % BLK_DEV)[:, None]
    return (local_block + ordering[:, :LIST]).astype(jnp.int32)


def draw_counts(key, part):
    brick_total = NBLOCKS // BLK_DEV
    brick_loads = jax.random.randint(jax.random.fold_in(key, 21), (brick_total,), 1, LIST + 1)
    busiest = jax.random.randint(jax.random.fold_in(key, 22), (), 0, brick_total)
    brick_loads = jnp.where(jnp.arange(brick_total, dtype=jnp.int32) == busiest, LIST, brick_loads)
    block_rows = jnp.arange(NBLOCKS, dtype=jnp.int32)
    lowered = brick_loads[block_rows // BLK_DEV] - jax.random.randint(jax.random.fold_in(key, 23), (NBLOCKS,), 0, 2)
    clipped = jnp.clip(lowered, 1, LIST)
    return jnp.where(block_rows == busiest * BLK_DEV, LIST, clipped).astype(jnp.int32)


def block_scale(stream_key, dims, split, least, top_value):
    loudness, own = 1.0, jax.random.fold_in(stream_key, 6)
    for axis_at, blocks in split:
        steps = jnp.exp(jax.random.uniform(jax.random.fold_in(own, axis_at), (blocks,), jnp.float32, least / len(split), top_value / len(split)))
        loudness = loudness * jnp.repeat(steps, dims[axis_at] // blocks).reshape([-1 if axis == axis_at else 1 for axis in range(len(dims))])
    return loudness


def centred(key, extent, width, reach, split=(), kind=jnp.bfloat16):
    drawn = jax.random.normal(key, extent, jnp.float32) * width
    if len(split) > 0:
        drawn = block_scale(key, extent, split, -0.22, 0.18) * drawn
    return jnp.clip(drawn, min=-reach, max=reach).astype(kind)


def setup_inputs(seed: int = 0) -> dict:
    key_list = jax.random.split(jax.random.key(seed), 10)
    features = centred(key_list[0], (C, ATOMS), 1.0, 6.0, ((0, 2), (1, 16)))
    positions = draw_positions(jax.random.fold_in(key_list[9], 71), 0)
    lists = draw_lists(jax.random.fold_in(key_list[9], 71), 0)
    counts = draw_counts(jax.random.fold_in(key_list[9], 71), 0)
    fourier_filter = jnp.clip(jnp.exp(math.log(4.0) - 2.0794415 * jax.random.uniform(key_list[4], (C, NK), jnp.float32) ** block_scale(key_list[4], (C, NK), ((0, 2),), -0.2, 0.2)), 0.5, 4.0)
    radial_weights = centred(key_list[5], (NBASIS, C), 0.3, 4.0, ((1, 2),), jnp.float32)
    norm_gain = jnp.clip(1.0 + 0.18 * jax.random.normal(key_list[6], (C,), jnp.float32), 0.1, 1.9)
    mlp_in = centred(key_list[7], (HID, C), C ** -0.5, 0.25, ((1, 2),))
    mlp_out = centred(key_list[8], (C, HID), HID ** -0.5, 0.1875, ((0, 2),))
    return {"features": features, "positions": positions, "lists": lists, "counts": counts, "fourier_filter": fourier_filter, "radial_weights": radial_weights, "norm_gain": norm_gain, "mlp_in": mlp_in, "mlp_out": mlp_out}


brick_width = 4.0
cross_width = 8.0
cutoff = 2.0
epsilon = 1e-06

def wave_table(side_count, brick_count):
    wave_index = jnp.arange(side_count ** 3, dtype=jnp.int32)
    first_number = (wave_index % side_count + 1).astype(jnp.float32)
    second_number = (wave_index // side_count % side_count - side_count // 2).astype(jnp.float32)
    third_number = (wave_index // (side_count * side_count) - side_count // 2).astype(jnp.float32)
    along_x = first_number * (2.0 * math.pi / (brick_count * brick_width))
    along_y = second_number * (2.0 * math.pi / cross_width)
    along_z = third_number * (2.0 * math.pi / cross_width)
    return (along_x, along_y, along_z)

def angle_rows(places, brick_float, along_x, along_y, along_z):
    x_place = (brick_float + places[0]) * brick_width
    y_place = places[1] * cross_width
    z_place = places[2] * cross_width
    return x_place[:, None] * along_x[None, :] + y_place[:, None] * along_y[None, :] + z_place[:, None] * along_z[None, :]

def phase_rows(places, brick_float, wave_vectors):
    angles = angle_rows(places, brick_float, wave_vectors[0], wave_vectors[1], wave_vectors[2])
    return jnp.concatenate([jnp.cos(angles), jnp.sin(angles)], axis=1).astype(jnp.bfloat16)

def radial_basis(delta_x, delta_y, delta_z, basis_count):
    squared = delta_x * delta_x + delta_y * delta_y + delta_z * delta_z
    distance = jnp.sqrt(squared)
    envelope = jnp.square(jnp.maximum(1.0 - squared / (cutoff * cutoff), 0.0))
    spacing = cutoff / (basis_count - 1)
    centres = (jnp.arange(basis_count, dtype=jnp.float32) * spacing).reshape((basis_count,) + (1,) * distance.ndim)
    scaled_gap = (distance[None] - centres) / spacing
    return (jnp.exp(-scaled_gap * scaled_gap) * envelope[None]).astype(jnp.bfloat16)

def reference(features, positions, lists, counts, fourier_filter, radial_weights, norm_gain, mlp_in, mlp_out):
    wave_vectors = wave_table(KSIDE, N_BRICK)
    inverse = 1.0 / math.sqrt(ATOMS)
    feature_bricks = jnp.transpose(features.reshape(C, N_BRICK, A_DEV), (1, 0, 2))
    place_bricks = jnp.transpose(positions.reshape(3, N_BRICK, A_DEV), (1, 0, 2))
    brick_ids = jnp.arange(N_BRICK, dtype=jnp.int32)

    def add_brick(partial_value, bundle):
        brick_id, feature_rows, places = bundle
        phases = phase_rows(places, brick_id.astype(jnp.float32), wave_vectors)
        return (partial_value + jnp.dot(feature_rows, phases, preferred_element_type=jnp.float32), None)
    partial_value, unused = lax.scan(add_brick, jnp.zeros((C, 2 * NK), jnp.float32), (brick_ids, feature_bricks, place_bricks))
    filtered = (jnp.concatenate([fourier_filter, fourier_filter], axis=1) * (partial_value * inverse)).astype(jnp.bfloat16)

    def evaluate(bundle):
        brick_id, places = bundle
        phases = phase_rows(places, brick_id.astype(jnp.float32), wave_vectors)
        return lax.dot_general(filtered, phases, (((1,), (1,)), ((), ())), preferred_element_type=jnp.float32) * inverse
    ewald = lax.map(evaluate, (brick_ids, place_bricks))
    ewald = jnp.transpose(ewald, (1, 0, 2)).reshape(C, ATOMS)
    feature_blocks = features.reshape(C, NBLOCKS, BLOCK)
    place_blocks = positions.reshape(3, NBLOCKS, BLOCK)

    def one_target(target):
        brick_id = target // BLK_DEV
        relative = lists[target] - REACH
        global_block = ((brick_id * BLK_DEV + relative) % NBLOCKS).astype(jnp.int32)
        offsets = (relative // BLK_DEV).astype(jnp.float32)
        source_places = jnp.take(place_blocks, global_block, axis=1)
        target_places = lax.dynamic_index_in_dim(place_blocks, target, 1, keepdims=False)
        source_x = source_places[0] + offsets[:, None]
        delta_x = (source_x[:, :, None] - target_places[0][None, None, :]) * brick_width
        delta_y = (source_places[1][:, :, None] - target_places[1][None, None, :]) * cross_width
        delta_z = (source_places[2][:, :, None] - target_places[2][None, None, :]) * cross_width
        radial_terms = radial_basis(delta_x, delta_y, delta_z, NBASIS)
        source_features = jnp.take(feature_blocks, global_block, axis=1)
        scaled = (source_features[:, :, None, :].astype(jnp.float32) * radial_weights.T[:, None, :, None]).astype(jnp.bfloat16)
        mask_weight = (jnp.arange(LIST, dtype=jnp.int32) < counts[target]).astype(jnp.float32)
        return jnp.einsum('clmb,mlba,l->ca', scaled.astype(jnp.float32), radial_terms.astype(jnp.float32), mask_weight)
    messages = lax.map(one_target, jnp.arange(NBLOCKS, dtype=jnp.int32))
    messages = jnp.transpose(messages, (1, 0, 2)).reshape(C, ATOMS)
    mixed = (features.astype(jnp.float32) + messages + ewald).astype(jnp.bfloat16)
    values = mixed.astype(jnp.float32)
    mean_square = lax.optimization_barrier(jnp.mean(values * values, axis=0, keepdims=True))
    normed = (values * lax.rsqrt(mean_square + epsilon) * norm_gain[:, None]).astype(jnp.bfloat16)
    hidden = jnp.dot(mlp_in, normed, preferred_element_type=jnp.float32)
    active = jax.nn.gelu(hidden).astype(jnp.bfloat16)
    return (values + jnp.dot(mlp_out, active, preferred_element_type=jnp.float32)).astype(jnp.bfloat16)
```

```python
import functools
import math

import jax
import jax.numpy as jnp
from jax import lax
from jax.experimental import pallas as pl
from jax.experimental.pallas import tpu as pltpu
from jax.sharding import PartitionSpec as P

KSIDE = 16
BLOCK = 128
REACH = 2
brick_width = 4.0
cross_width = 8.0
cutoff = 2.0
epsilon = 1e-06

HALF = KSIDE // 2
PLANE = KSIDE * KSIDE
PLACE_ROWS = 8
VMEM_LIMIT = 60 * 1024 * 1024
NT = (((1,), (1,)), ((), ()))

SIN_TERMS = [(-1) ** n / math.factorial(2 * n + 1) for n in range(7)]
COS_TERMS = [(-1) ** n / math.factorial(2 * n) for n in range(8)]


def horner(terms, squared):
    value = jnp.full_like(squared, terms[-1])
    for term in terms[-2::-1]:
        value = value * squared + term
    return value


def turn_cos_sin(turns):
    half = (turns - jnp.round(turns)) * math.pi
    squared = half * half
    sine = half * horner(SIN_TERMS, squared)
    cosine = horner(COS_TERMS, squared)
    return 1.0 - 2.0 * sine * sine, 2.0 * sine * cosine


def read_places(rows):
    rows = rows.astype(jnp.float32)
    first = rows[0:1] + rows[1:2]
    second = rows[2:3] + rows[3:4] + rows[4:5]
    third = rows[5:6] + rows[6:7] + rows[7:8]
    return first, second, third


def split_places(positions, blocks_dev):
    atom_count = positions.shape[1]
    own_block = (jnp.arange(atom_count, dtype=jnp.int32) // BLOCK).astype(jnp.float32)
    rest = [positions[0] * blocks_dev - own_block, positions[1], positions[2]]
    rows = []
    for value, pieces in zip(rest, (2, 3, 3)):
        for _ in range(pieces):
            piece = lax.reduce_precision(value, 8, 7)
            rows.append(piece)
            value = value - piece
    return jnp.stack(rows).astype(jnp.bfloat16)


def ewald_kernel(gathered, filters, out, table, depth_table, scaled, sums, weights, *, halves):
    bricks, rows_in, atom_count = gathered.shape
    channels = rows_in - PLACE_ROWS
    blocks_dev = atom_count // BLOCK
    total = bricks * atom_count
    inverse = 1.0 / math.sqrt(total)
    lane_block = lax.broadcasted_iota(jnp.int32, (1, atom_count), 1) // BLOCK
    lane_block = lane_block.astype(jnp.float32)
    wave = lax.broadcasted_iota(jnp.int32, (KSIDE, 1), 0).astype(jnp.float32) + 1.0
    mid_wave = lax.broadcasted_iota(jnp.int32, (HALF, 1), 0).astype(jnp.float32) + 0.5

    def columns(brick):
        return pl.ds(pl.multiple_of(brick * atom_count, atom_count), atom_count)

    def make_tables(brick, slot):
        cols = columns(brick)
        first, second, third = read_places(gathered[brick, channels:, :])
        along = (jnp.float32(1.0) * (brick * blocks_dev) + lane_block + first) * (
            1.0 / (blocks_dev * bricks)
        )
        x_cos, x_sin = turn_cos_sin(wave * along - 0.5 * (second + third))
        y_cos, y_sin = turn_cos_sin(mid_wave * second)
        z_cos, z_sin = turn_cos_sin(mid_wave * third)
        depth_table[0:HALF, cols] = z_cos
        depth_table[HALF:KSIDE, cols] = z_sin
        for k in range(HALF):
            cos_row, sin_row = y_cos[k : k + 1], y_sin[k : k + 1]
            a, b = x_cos * cos_row, x_sin * sin_row
            c, d = x_sin * cos_row, x_cos * sin_row
            above, below = (HALF + k) * KSIDE, (HALF - 1 - k) * KSIDE
            table[pl.ds(above, KSIDE), cols] = (a - b).astype(jnp.bfloat16)
            table[pl.ds(PLANE + above, KSIDE), cols] = (c + d).astype(jnp.bfloat16)
            table[pl.ds(below, KSIDE), cols] = (a + b).astype(jnp.bfloat16)
            table[pl.ds(PLANE + below, KSIDE), cols] = (c - d).astype(jnp.bfloat16)
        values = gathered[brick, 0:channels, :].astype(jnp.float32)
        for k in range(HALF):
            scaled[slot, pl.ds(k * channels, channels), :] = (values * z_cos[k : k + 1]).astype(
                jnp.bfloat16
            )
            scaled[slot, pl.ds((HALF + k) * channels, channels), :] = (
                values * z_sin[k : k + 1]
            ).astype(jnp.bfloat16)

    sums[...] = jnp.zeros_like(sums)

    @pl.loop(0, bricks)
    def _(brick):
        make_tables(brick, 0)
        sums[...] += lax.dot_general(
            scaled[0], table[:, columns(brick)], NT, preferred_element_type=jnp.float32
        )

    for k in range(HALF):
        upper = filters[:, pl.ds((HALF + k) * PLANE, PLANE)]
        lower = filters[:, pl.ds((HALF - 1 - k) * PLANE, PLANE)]
        both, apart = (upper + lower) * inverse, (upper - lower) * inverse
        cos_rows = pl.ds(k * channels, channels)
        sin_rows = pl.ds((HALF + k) * channels, channels)
        cos_real, cos_imag = sums[cos_rows, 0:PLANE], sums[cos_rows, PLANE:]
        sin_real, sin_imag = sums[sin_rows, 0:PLANE], sums[sin_rows, PLANE:]
        weights[cos_rows, 0:PLANE] = (both * cos_real - apart * sin_imag).astype(jnp.bfloat16)
        weights[cos_rows, PLANE:] = (both * cos_imag + apart * sin_real).astype(jnp.bfloat16)
        weights[sin_rows, 0:PLANE] = (apart * cos_imag + both * sin_real).astype(jnp.bfloat16)
        weights[sin_rows, PLANE:] = (both * sin_imag - apart * cos_real).astype(jnp.bfloat16)

    @pl.loop(0, bricks)
    def _(brick):
        cols = columns(brick)
        mixed = jnp.dot(weights[...], table[:, cols], preferred_element_type=jnp.float32)
        depth = depth_table[:, cols]
        value = mixed[0:channels] * depth[0:1]
        for k in range(1, KSIDE):
            value = value + mixed[k * channels : (k + 1) * channels] * depth[k : k + 1]
        value = (value * inverse).astype(jnp.bfloat16)
        width = atom_count // halves
        for part in range(halves):
            out[brick * halves + part] = value[:, part * width : (part + 1) * width]


def ewald_call(gathered, filters, halves):
    bricks, rows_in, atom_count = gathered.shape
    channels = rows_in - PLACE_ROWS
    total = bricks * atom_count
    return pl.pallas_call(
        functools.partial(ewald_kernel, halves=halves),
        out_shape=jax.ShapeDtypeStruct(
            (bricks * halves, channels, atom_count // halves), jnp.bfloat16
        ),
        scratch_shapes=[
            pltpu.VMEM((2 * PLANE, total), jnp.bfloat16),
            pltpu.VMEM((KSIDE, total), jnp.float32),
            pltpu.VMEM((2, KSIDE * channels, atom_count), jnp.bfloat16),
            pltpu.VMEM((KSIDE * channels, 2 * PLANE), jnp.float32),
            pltpu.VMEM((KSIDE * channels, 2 * PLANE), jnp.bfloat16),
        ],
        compiler_params=pltpu.CompilerParams(vmem_limit_bytes=VMEM_LIMIT),
        cost_estimate=pl.CostEstimate(
            flops=8 * KSIDE * channels * PLANE * total,
            bytes_accessed=gathered.size * 2 + filters.size * 4,
            transcendentals=0,
        ),
        name="ewald",
    )(gathered, filters)


def message_kernel(
    info, lists, counts, gathered, targets, *refs, parts, base_slots, halo_slots, basis_count
):
    own_refs, halo_refs = refs[:parts], refs[parts : 2 * parts]
    weight_refs = refs[2 * parts : 3 * parts]
    out, scaled, basis = refs[3 * parts :]
    own_blocks = own_refs[0].shape[1] // BLOCK
    halo_blocks = halo_refs[0].shape[1] // BLOCK
    part_rows = own_refs[0].shape[0]
    target_total = out.shape[1]
    tile = min(BLOCK, target_total)
    bricks = gathered.shape[0]
    places_at = gathered.shape[1] - PLACE_ROWS
    spacing = cutoff / (basis_count - 1)
    brick, chan, first_window, own_slot = info[0], info[1], info[2], info[3]
    step = 16

    for part in range(parts):

        @pl.loop(0, part_rows // step)
        def _(group):
            rows = pl.ds(pl.multiple_of(group * step, step), step)
            gains = [
                jnp.broadcast_to(weight_refs[part][rows, m : m + 1], (step, BLOCK))
                for m in range(basis_count)
            ]
            target_rows = pl.ds(pl.multiple_of(part * part_rows + group * step, step), step)
            for ref, block_total, slot_at in (
                (own_refs[part], own_blocks, None),
                (halo_refs[part], halo_blocks, 4),
            ):
                for block in range(block_total):
                    slot = own_slot + block if slot_at is None else info[slot_at + block]
                    value = ref[rows, block * BLOCK : (block + 1) * BLOCK].astype(jnp.float32)
                    for m in range(basis_count):
                        scaled[slot, target_rows, m * BLOCK : (m + 1) * BLOCK] = (
                            value * gains[m]
                        ).astype(jnp.bfloat16)

    first_target = chan * target_total
    for tile_index in range(target_total // tile):
        rows = pl.ds(tile_index * tile, tile)
        target_block = (first_target + tile_index * tile) // BLOCK
        x_target, y_target, z_target = targets[0, rows], targets[1, rows], targets[2, rows]
        out_lanes = pl.ds(tile_index * tile, tile)
        for part in range(parts):
            part_slice = pl.ds(part * part_rows, part_rows)
            own = own_refs[part][:, pl.ds(pl.multiple_of(first_target, tile) + tile_index * tile, tile)] if target_total % BLOCK == 0 else targets_slice(own_refs[part], first_target, tile)
            out[part_slice, out_lanes] = own.astype(jnp.float32)

        @pl.loop(0, counts[target_block])
        def _(entry):
            listed = lists[target_block * (lists.shape[0] // counts.shape[0]) + entry]
            shift = listed + own_blocks - REACH
            source_brick = lax.rem(brick + shift // own_blocks - 1 + bricks, bricks)
            lanes = pl.ds(pl.multiple_of(lax.rem(shift, own_blocks) * BLOCK, BLOCK), BLOCK)
            first, second, third = read_places(gathered[source_brick, places_at:, lanes])
            first = (first + (listed - REACH).astype(jnp.float32)) * (1.0 / own_blocks)
            dx = (first - x_target) * brick_width
            dy = (second - y_target) * cross_width
            dz = (third - z_target) * cross_width
            squared = dx * dx + dy * dy + dz * dz
            distance = jnp.sqrt(squared)
            envelope = jnp.maximum(1.0 - squared / (cutoff * cutoff), 0.0)
            envelope = envelope * envelope
            for m in range(basis_count):
                gap = distance * (1.0 / spacing) - m
                basis[:, m * BLOCK : (m + 1) * BLOCK] = (
                    jnp.exp(-gap * gap) * envelope
                ).astype(jnp.bfloat16)
            out[:, out_lanes] += lax.dot_general(
                scaled[listed - first_window], basis[...], NT, preferred_element_type=jnp.float32
            )


def targets_slice(ref, first, width):
    value = ref[...]
    total = value.shape[1]
    picked = value[:, 0:width]
    for start in range(width, total, width):
        picked = jnp.where(first == start, value[:, start : start + width], picked)
    return picked


def message_call(info, lists, counts, gathered, targets, owns, halos, gains, basis_count):
    parts = len(owns)
    part_rows, atom_count = owns[0].shape
    slots = (atom_count + halos[0].shape[1]) // BLOCK
    target_total = targets.shape[1]
    tile = min(BLOCK, target_total)
    smem = pl.BlockSpec(memory_space=pltpu.SMEM)
    vmem = pl.BlockSpec(memory_space=pltpu.VMEM)
    channels = parts * part_rows
    return pl.pallas_call(
        functools.partial(
            message_kernel, parts=parts, base_slots=0, halo_slots=0, basis_count=basis_count
        ),
        out_shape=jax.ShapeDtypeStruct((channels, target_total), jnp.float32),
        in_specs=[smem] * 3 + [vmem] * (2 + 3 * parts),
        out_specs=vmem,
        scratch_shapes=[
            pltpu.VMEM((slots, channels, basis_count * BLOCK), jnp.bfloat16),
            pltpu.VMEM((tile, basis_count * BLOCK), jnp.bfloat16),
        ],
        compiler_params=pltpu.CompilerParams(vmem_limit_bytes=VMEM_LIMIT),
        cost_estimate=pl.CostEstimate(
            flops=8 * channels * basis_count * BLOCK * target_total,
            bytes_accessed=channels * target_total * 8,
            transcendentals=0,
        ),
        name="messages",
    )(info, lists, counts, gathered, targets, *owns, *halos, *gains)


def mixing_kernel(info, base, ewald, gain, *refs, parts, per_device):
    in_refs, out_refs = refs[:parts], refs[parts : 2 * parts]
    out, mixed, normed, active = refs[2 * parts :]
    channels, width = base.shape
    part_rows = channels // parts
    chan = info[1]
    squares = jnp.zeros((1, width), jnp.float32)
    for part in range(parts):
        other = lax.rem(chan + part, parts)
        for start in range(0, part_rows, per_device):
            rows = pl.ds(part * part_rows + start, per_device)
            piece = ewald[(start // per_device) * parts + other].astype(jnp.float32)
            value = (base[rows] + piece).astype(jnp.bfloat16).astype(jnp.float32)
            mixed[rows] = value
            squares = squares + jnp.sum(value * value, axis=0, keepdims=True)
    factor = lax.rsqrt(squares * (1.0 / channels) + epsilon)
    for part in range(parts):
        other = lax.rem(chan + part, parts)
        rows = pl.ds(part * part_rows, part_rows)
        here = pl.ds(pl.multiple_of(other * part_rows, part_rows), part_rows)
        normed[rows] = (mixed[rows] * factor * gain[here]).astype(jnp.bfloat16)
    hidden_total = in_refs[0].shape[0]
    step = 256
    for start in range(0, hidden_total, step):
        rows = pl.ds(start, step)
        hidden = jnp.dot(
            in_refs[0][rows], normed[0:part_rows], preferred_element_type=jnp.float32
        )
        for part in range(1, parts):
            hidden = hidden + jnp.dot(
                in_refs[part][rows],
                normed[part * part_rows : (part + 1) * part_rows],
                preferred_element_type=jnp.float32,
            )
        active[rows] = jax.nn.gelu(hidden).astype(jnp.bfloat16)
    for part in range(parts):
        other = lax.rem(chan + part, parts)
        here = pl.ds(pl.multiple_of(other * part_rows, part_rows), part_rows)
        value = jnp.dot(out_refs[part][...], active[...], preferred_element_type=jnp.float32)
        out[here] = (mixed[pl.ds(part * part_rows, part_rows)] + value).astype(jnp.bfloat16)


def mixing_call(info, base, ewald, gain, ins, outs):
    parts = len(ins)
    channels, width = base.shape
    hidden = ins[0].shape[0]
    smem = pl.BlockSpec(memory_space=pltpu.SMEM)
    vmem = pl.BlockSpec(memory_space=pltpu.VMEM)
    return pl.pallas_call(
        functools.partial(mixing_kernel, parts=parts, per_device=ewald.shape[1]),
        out_shape=jax.ShapeDtypeStruct((channels, width), jnp.bfloat16),
        in_specs=[smem] + [vmem] * (3 + 2 * parts),
        out_specs=vmem,
        scratch_shapes=[
            pltpu.VMEM((channels, width), jnp.float32),
            pltpu.VMEM((channels, width), jnp.bfloat16),
            pltpu.VMEM((hidden, width), jnp.bfloat16),
        ],
        compiler_params=pltpu.CompilerParams(vmem_limit_bytes=VMEM_LIMIT),
        cost_estimate=pl.CostEstimate(
            flops=4 * channels * hidden * width,
            bytes_accessed=4 * channels * hidden,
            transcendentals=hidden * width,
        ),
        name="mixing",
    )(info, base, ewald, gain, *ins, *outs)


def chan_parts(value, count):
    return [value] + [
        lax.ppermute(value, "chan", [((i + part) % count, i) for i in range(count)])
        for part in range(1, count)
    ]


def body(
    features, positions, lists, counts, fourier_filter, radial_weights, norm_gain, mlp_in, mlp_out
):
    part_rows, atom_count = features.shape
    bricks, chans = lax.axis_size("brick"), lax.axis_size("chan")
    brick, chan = lax.axis_index("brick"), lax.axis_index("chan")
    blocks_dev = atom_count // BLOCK
    basis_count = radial_weights.shape[0]
    per_device = part_rows // bricks
    padded = -(-per_device // 16) * 16
    width = atom_count // chans
    rim = blocks_dev // 2 * BLOCK

    sent = features.reshape(bricks, per_device, atom_count)
    if padded != per_device:
        sent = jnp.pad(sent, ((0, 0), (0, padded - per_device), (0, 0)))
    place_rows = split_places(positions, blocks_dev)
    sent = jnp.concatenate(
        [sent, jnp.broadcast_to(place_rows[None], (bricks, PLACE_ROWS, atom_count))], axis=1
    )
    gathered = lax.all_to_all(sent, "brick", 0, 0)

    filters = lax.dynamic_slice_in_dim(fourier_filter, brick * per_device, per_device, 0)
    if padded != per_device:
        filters = jnp.pad(filters, ((0, padded - per_device), (0, 0)))
    halves = chans if width % BLOCK == 0 else 1
    ewald = ewald_call(gathered, filters, halves)
    ewald = ewald[:, :per_device]
    if halves != chans:
        ewald = ewald.reshape(bricks, per_device, chans, width)
        ewald = ewald.transpose(0, 2, 1, 3).reshape(bricks * chans, per_device, width)
    arrived = lax.all_to_all(ewald, ("brick", "chan"), 0, 0)

    owns = chan_parts(features, chans)
    gains = chan_parts(radial_weights.T, chans)
    head = features[:, :rim]
    tail = features[:, atom_count - rim :]
    if chans == 2 and blocks_dev == 2 * REACH:
        lower = chan == 0
        names = ("brick", "chan")

        def source(low_from, high_from):
            pairs = []
            for i in range(bricks):
                pairs.append((((i - 1) % bricks) * 2 + low_from, i * 2))
                pairs.append((((i + 1) % bricks) * 2 + high_from, i * 2 + 1))
            return pairs

        first = jnp.where(lower, tail, head)
        second = jnp.where(lower, head, tail)
        halos = [
            lax.ppermute(first, names, source(0, 1)),
            lax.ppermute(second, names, source(1, 0)),
        ]
        own_slot = jnp.where(lower, REACH, 0)
        halo_slots = [jnp.where(lower, i, blocks_dev + i) for i in range(REACH)]
        first_window = jnp.where(lower, 0, REACH)
    else:
        before = lax.ppermute(tail, "brick", [(i, (i + 1) % bricks) for i in range(bricks)])
        after = lax.ppermute(head, "brick", [((i + 1) % bricks, i) for i in range(bricks)])
        halos = chan_parts(jnp.concatenate([before, after], axis=1), chans)
        own_slot = rim // BLOCK
        halo_slots = [i for i in range(rim // BLOCK)]
        halo_slots += [rim // BLOCK + blocks_dev + i for i in range(rim // BLOCK)]
        first_window = 0
    info = jnp.stack(
        [jnp.asarray(v, jnp.int32) for v in [brick, chan, first_window, own_slot, *halo_slots]]
    )
    own_places = lax.dynamic_slice_in_dim(positions, chan * width, width, 1)
    targets = jnp.broadcast_to(own_places[:, :, None], (3, width, BLOCK))
    base = message_call(
        info, lists.reshape(-1), counts, gathered, targets, owns, halos, gains, basis_count
    )

    ins = chan_parts(mlp_in, chans)
    outs = chan_parts(mlp_out, chans)
    return mixing_call(info, base, arrived, norm_gain[:, None], ins, outs)


def solution(mesh):
    placed = (
        P("chan", "brick"),
        P(None, "brick"),
        P("brick", None),
        P("brick"),
        P("chan", None),
        P(None, "chan"),
        P(),
        P(None, "chan"),
        P("chan", None),
    )
    return jax.shard_map(
        body, mesh=mesh, in_specs=placed, out_specs=P(None, ("brick", "chan")), check_vma=False
    )
```

```python
import functools
import math

import jax
import jax.numpy as jnp
from jax import lax
from jax.experimental import pallas as pl
from jax.experimental.pallas import tpu as pltpu
from jax.sharding import PartitionSpec as P


KSIDE = 16
BLOCK = 128
REACH = 2
brick_width = 4.0
cross_width = 8.0
cutoff = 2.0
epsilon = 1e-06

HALF = KSIDE // 2
PLANE = KSIDE * KSIDE
PLACE_ROWS = 8
LANES = 128
SMALL_LIMIT = 4 * 1024 * 1024
NT = (((1,), (1,)), ((), ()))

SIN_TERMS = (3.14159258, -5.1677069, 2.55003164, -0.59804645, 0.07722225)
COS_TERMS = (0.99999995, -4.93479286, 4.05841191, -1.33188016, 0.2196968)


def horner(terms, squared):
    value = squared * terms[-1] + terms[-2]
    for term in terms[-3::-1]:
        value = value * squared + term
    return value


def turn_cos_sin(turns):
    near = turns - jnp.round(turns)
    squared = near * near
    sine = near * horner(SIN_TERMS, squared)
    double = sine + sine
    return 1.0 - double * sine, double * horner(COS_TERMS, squared)


def same_row(ref, row, count):
    return ref[pl.ds(row, count, stride=0), :]


def read_places(ref, count):
    first = same_row(ref, 0, count) + same_row(ref, 3, count)
    second = same_row(ref, 1, count) + same_row(ref, 4, count) + same_row(ref, 6, count)
    third = same_row(ref, 2, count) + same_row(ref, 5, count) + same_row(ref, 7, count)
    return first, second, third


def split_places(positions, blocks_dev):
    atom_count = positions.shape[1]
    own_block = (jnp.arange(atom_count, dtype=jnp.int32) // BLOCK).astype(jnp.float32)
    rest = jnp.stack([positions[0] * blocks_dev - own_block, positions[1], positions[2]])
    pieces = []
    for _ in range(3):
        piece = lax.reduce_precision(rest, 8, 7)
        pieces.append(piece)
        rest = rest - piece
    pieces[2] = pieces[2][1:]
    return jnp.concatenate(pieces).astype(jnp.bfloat16)


def pack_kernel(features, positions, out, rows):
    bricks, rows_out, atom_count = out.shape
    per_device = rows_out - PLACE_ROWS
    blocks_dev = atom_count // BLOCK
    own_block = lax.broadcasted_iota(jnp.int32, (1, atom_count), 1) // BLOCK
    rows[0:1] = positions[0:1] * blocks_dev - own_block.astype(jnp.float32)
    rows[1:3] = positions[1:3]
    rest = rows[0:3]
    high = rest.astype(jnp.bfloat16).astype(jnp.float32)
    rest = rest - high
    middle = rest.astype(jnp.bfloat16).astype(jnp.float32)
    rest = rest - middle
    rows[0:3] = high
    rows[3:6] = middle
    rows[6:8] = rest[1:3]
    places = rows[...].astype(jnp.bfloat16)
    for device in range(bricks):
        out[device, 0:per_device] = features[device * per_device : (device + 1) * per_device]
        out[device, per_device:] = places


def pack_call(features, positions, bricks):
    per_device = features.shape[0] // bricks
    atom_count = features.shape[1]
    return pl.pallas_call(
        pack_kernel,
        out_shape=jax.ShapeDtypeStruct(
            (bricks, per_device + PLACE_ROWS, atom_count), jnp.bfloat16
        ),
        scratch_shapes=[pltpu.VMEM((PLACE_ROWS, atom_count), jnp.float32)],
        compiler_params=pltpu.CompilerParams(vmem_limit_bytes=SMALL_LIMIT),
        name="pack",
    )(features, positions)


def ewald_kernel(
    info,
    gathered,
    filters,
    out,
    near,
    places,
    table,
    y_table,
    depth_table,
    scaled,
    sums,
    weights,
    *,
    halves,
):
    bricks, rows_in, atom_count = gathered.shape
    channels = rows_in - PLACE_ROWS
    groups = atom_count // LANES
    total = bricks * atom_count
    blocks_dev = atom_count // BLOCK
    inverse = 1.0 / math.sqrt(total)
    lane_block = lax.broadcasted_iota(jnp.int32, (1, atom_count), 1) // BLOCK
    lane_block = lane_block.astype(jnp.float32)
    wave = lax.broadcasted_iota(jnp.int32, (HALF, 1), 0).astype(jnp.float32) + 1.0
    mid_wave = wave - 0.5

    def make_tables(brick, slot):
        places[slot] = gathered[brick, channels:, :].astype(jnp.float32)
        first, second, third = read_places(places.at[slot], HALF)
        start = (brick * blocks_dev).astype(jnp.float32) + lane_block
        along = (first + start) * (1.0 / (blocks_dev * bricks))
        centre = 0.5 * (second + third)
        low_cos, low_sin = turn_cos_sin(wave * along - centre)
        high_cos, high_sin = turn_cos_sin((wave + HALF) * along - centre)
        y_cos, y_sin = turn_cos_sin(mid_wave * second)
        z_cos, z_sin = turn_cos_sin(mid_wave * third)
        for group in range(groups):
            lanes = slice(group * LANES, (group + 1) * LANES)
            y_ref, z_ref = y_table.at[slot, group], depth_table.at[brick, group]
            y_ref[0:HALF] = y_cos[:, lanes]
            y_ref[HALF:] = y_sin[:, lanes]
            z_ref[0:HALF] = z_cos[:, lanes]
            z_ref[HALF:] = z_sin[:, lanes]
            here = brick * groups + group
            x_cos = jnp.concatenate([low_cos[:, lanes], high_cos[:, lanes]], axis=0)
            x_sin = jnp.concatenate([low_sin[:, lanes], high_sin[:, lanes]], axis=0)
            for k in range(HALF):
                cos_row = same_row(y_ref, k, KSIDE)
                sin_row = same_row(y_ref, HALF + k, KSIDE)
                a, b = x_cos * cos_row, x_sin * sin_row
                c, d = x_sin * cos_row, x_cos * sin_row
                above, below = (HALF + k) * KSIDE, (HALF - 1 - k) * KSIDE
                table[here, above : above + KSIDE] = (a - b).astype(jnp.bfloat16)
                table[here, PLANE + above : PLANE + above + KSIDE] = (c + d).astype(jnp.bfloat16)
                table[here, below : below + KSIDE] = (a + b).astype(jnp.bfloat16)
                table[here, PLANE + below : PLANE + below + KSIDE] = (c - d).astype(jnp.bfloat16)
            values = gathered[brick, 0:channels, lanes].astype(jnp.float32)
            for k in range(KSIDE):
                factor = same_row(z_ref, k, channels)
                scaled[slot, group, k * channels : (k + 1) * channels] = (values * factor).astype(
                    jnp.bfloat16
                )

    def table_of(brick):
        return jnp.concatenate([table[brick * groups + group] for group in range(groups)], axis=1)

    def add_sums(brick, slot):
        rows = jnp.concatenate([scaled[slot, group] for group in range(groups)], axis=1)
        sums[...] += lax.dot_general(rows, table_of(brick), NT, preferred_element_type=jnp.float32)

    sums[...] = jnp.zeros_like(sums)
    for step in range(3):
        neighbour = lax.rem(info[0] + (step - 1 + bricks), bricks)
        rows = gathered[neighbour, channels:, :].astype(jnp.float32)
        for block in range(blocks_dev):
            near[step * blocks_dev + block] = rows[:, block * BLOCK : (block + 1) * BLOCK]

    pairs = (bricks - 1) // 2
    make_tables(jnp.int32(0), 0)

    @pl.loop(0, pairs)
    def _(pair):
        add_sums(2 * pair, 0)
        make_tables(2 * pair + 1, 1)
        add_sums(2 * pair + 1, 1)
        make_tables(2 * pair + 2, 0)

    for brick in range(2 * pairs, bricks):
        add_sums(brick, brick % 2)
        if brick + 1 < bricks:
            make_tables(jnp.int32(brick + 1), (brick + 1) % 2)

    for k in range(HALF):
        upper = filters[:, pl.ds((HALF + k) * PLANE, PLANE)]
        lower = filters[:, pl.ds((HALF - 1 - k) * PLANE, PLANE)]
        both, apart = (upper + lower) * inverse, (upper - lower) * inverse
        cos_rows = pl.ds(k * channels, channels)
        sin_rows = pl.ds((HALF + k) * channels, channels)
        cos_real, cos_imag = sums[cos_rows, 0:PLANE], sums[cos_rows, PLANE:]
        sin_real, sin_imag = sums[sin_rows, 0:PLANE], sums[sin_rows, PLANE:]
        for row_part, first_part, value in (
            (cos_rows, 0, both * cos_real - apart * sin_imag),
            (cos_rows, PLANE, both * cos_imag + apart * sin_real),
            (sin_rows, 0, apart * cos_imag + both * sin_real),
            (sin_rows, PLANE, both * sin_imag - apart * cos_real),
        ):
            value = value.astype(jnp.bfloat16)
            for at in range(0, PLANE, LANES):
                weights[(first_part + at) // LANES, row_part] = value[:, at : at + LANES]

    @pl.loop(0, bricks, unroll=8)
    def _(brick):
        rows = jnp.concatenate([weights[at] for at in range(2 * PLANE // LANES)], axis=1)
        mixed = jnp.dot(rows, table_of(brick), preferred_element_type=jnp.float32)
        values = []
        for group in range(groups):
            z_ref = depth_table.at[brick, group]
            lanes = slice(group * LANES, (group + 1) * LANES)
            value = mixed[0:channels, lanes] * same_row(z_ref, 0, channels)
            for k in range(1, KSIDE):
                part = mixed[k * channels : (k + 1) * channels, lanes]
                value = value + part * same_row(z_ref, k, channels)
            values.append(value)
        value = jnp.concatenate(values, axis=1)
        value = (value * inverse).astype(jnp.bfloat16)
        width = atom_count // halves
        for part in range(halves):
            out[brick * halves + part] = value[:, part * width : (part + 1) * width]


def bytes_of(*shapes):
    total = 0
    for shape, dtype in shapes:
        padded = [*shape[:-2], -(-shape[-2] // 16) * 16, -(-shape[-1] // LANES) * LANES]
        total += math.prod(padded) * jnp.dtype(dtype).itemsize
    return total


def ewald_call(info, gathered, filters, halves):
    bricks, rows_in, atom_count = gathered.shape
    channels = rows_in - PLACE_ROWS
    total = bricks * atom_count
    rows = KSIDE * channels
    scratch = [
        ((2, PLACE_ROWS, atom_count), jnp.float32),
        ((total // LANES, 2 * PLANE, LANES), jnp.bfloat16),
        ((2, atom_count // LANES, KSIDE, LANES), jnp.float32),
        ((bricks, atom_count // LANES, KSIDE, LANES), jnp.float32),
        ((2, atom_count // LANES, rows, LANES), jnp.bfloat16),
        ((rows, 2 * PLANE), jnp.float32),
        ((2 * PLANE // LANES, rows, LANES), jnp.bfloat16),
    ]
    out = ((bricks * halves, channels, atom_count // halves), jnp.bfloat16)
    near = ((3 * atom_count // BLOCK, PLACE_ROWS, BLOCK), jnp.float32)
    held = [out, near, (gathered.shape, gathered.dtype), (filters.shape, filters.dtype)]
    smem, vmem = pl.BlockSpec(memory_space=pltpu.SMEM), pl.BlockSpec(memory_space=pltpu.VMEM)
    return pl.pallas_call(
        functools.partial(ewald_kernel, halves=halves),
        out_shape=(jax.ShapeDtypeStruct(*out), jax.ShapeDtypeStruct(*near)),
        in_specs=[smem, vmem, vmem],
        out_specs=(vmem, vmem),
        scratch_shapes=[pltpu.VMEM(*entry) for entry in scratch],
        compiler_params=pltpu.CompilerParams(
            vmem_limit_bytes=bytes_of(*scratch, *held) + SMALL_LIMIT
        ),
        cost_estimate=pl.CostEstimate(
            flops=8 * rows * PLANE * total,
            bytes_accessed=gathered.size * 2 + filters.size * 4,
            transcendentals=0,
        ),
        name="ewald",
    )(info, gathered, filters)


def message_kernel(info, lists, counts, near, positions, *refs, parts, basis_count):
    own_refs, halo_refs = refs[:parts], refs[parts : 2 * parts]
    weight_refs = refs[2 * parts : 3 * parts]
    out, scaled = refs[3 * parts :]
    part_rows, atom_count = own_refs[0].shape
    own_blocks = atom_count // BLOCK
    halo_blocks = halo_refs[0].shape[1] // BLOCK
    channels, target_total = out.shape
    tile = min(BLOCK, target_total)
    spacing = cutoff / (basis_count - 1)
    root = math.sqrt(math.log2(math.e))
    chan, first_window, own_slot = info[1], info[2], info[3]
    step = 16
    listed_total = lists.shape[0] // counts.shape[0]

    for part in range(parts):

        @pl.loop(0, part_rows // step)
        def _(group):
            rows = pl.ds(pl.multiple_of(group * step, step), step)
            gains = [
                jnp.broadcast_to(weight_refs[part][rows, m : m + 1], (step, BLOCK))
                for m in range(basis_count)
            ]
            into = pl.ds(pl.multiple_of(part * part_rows + group * step, step), step)
            blocks = [(own_refs[part], i, own_slot + i) for i in range(own_blocks)]
            blocks += [(halo_refs[part], i, info[5 + i]) for i in range(halo_blocks)]
            for ref, block, slot in blocks:
                value = ref[rows, block * BLOCK : (block + 1) * BLOCK].astype(jnp.float32)
                for m in range(basis_count):
                    scaled[slot, m, into] = (value * gains[m]).astype(jnp.bfloat16)

    first_target = chan * target_total
    for start in range(0, target_total, tile):
        target_block = (first_target + start) // BLOCK
        places = own_tile(positions, first_target, start, tile)
        places = jnp.concatenate([places, jnp.zeros((8 - 3, tile), jnp.float32)]).T
        x_target, y_target, z_target = (
            jnp.broadcast_to(places[:, axis : axis + 1] * scale, (tile, BLOCK))
            for axis, scale in enumerate((brick_width, cross_width, cross_width))
        )

        def add_entry(entry, running):
            listed = lists[target_block * listed_total + entry]
            first, second, third = read_places(near.at[listed + (own_blocks - REACH)], 8)
            first = (first + (listed - REACH).astype(jnp.float32)) * (brick_width / own_blocks)
            second, third = second * cross_width, third * cross_width
            dx = jnp.concatenate([first] * (tile // 8)) - x_target
            dy = jnp.concatenate([second] * (tile // 8)) - y_target
            dz = jnp.concatenate([third] * (tile // 8)) - z_target
            squared = dx * dx + dy * dy + dz * dz
            reach = jnp.sqrt(squared) * (root / spacing)
            envelope = jnp.maximum(1.0 - squared * (1.0 / (cutoff * cutoff)), 0.0)
            envelope = envelope * envelope
            basis = []
            for m in range(basis_count):
                gap = reach - m * root
                basis.append((jnp.exp2(-(gap * gap)) * envelope).astype(jnp.bfloat16))
            source = scaled.at[listed - first_window]
            return running + lax.dot_general(
                jnp.concatenate(basis, axis=1),
                jnp.concatenate([source[m] for m in range(basis_count)], axis=1),
                NT,
                preferred_element_type=jnp.float32,
            )

        summed = lax.fori_loop(
            0, counts[target_block], add_entry, jnp.zeros((tile, channels), jnp.float32)
        )
        summed = summed.T
        for part in range(parts):
            own = own_tile(own_refs[part], first_target, start, tile)
            out[pl.ds(part * part_rows, part_rows), start : start + tile] = (
                own.astype(jnp.float32) + summed[part * part_rows : (part + 1) * part_rows]
            )


def own_tile(ref, first, start, width):
    if width % LANES == 0:
        return ref[:, pl.ds(pl.multiple_of(first + start, LANES), width)]
    value = ref[...]
    picked = value[:, 0:width]
    for at in range(width, value.shape[1], width):
        picked = jnp.where(first + start == at, value[:, at : at + width], picked)
    return picked


def message_call(info, lists, counts, near, positions, owns, halos, gains, basis_count):
    parts = len(owns)
    part_rows, atom_count = owns[0].shape
    slots = (atom_count + halos[0].shape[1]) // BLOCK
    target_total = atom_count // parts
    smem = pl.BlockSpec(memory_space=pltpu.SMEM)
    vmem = pl.BlockSpec(memory_space=pltpu.VMEM)
    channels = parts * part_rows
    operands = [near, positions, *owns, *halos, *gains]
    scratch = [((slots, basis_count, channels, BLOCK), jnp.bfloat16)]
    out = ((channels, target_total), jnp.float32)
    held = [out, *((value.shape, value.dtype) for value in operands)]
    return pl.pallas_call(
        functools.partial(message_kernel, parts=parts, basis_count=basis_count),
        out_shape=jax.ShapeDtypeStruct(*out),
        in_specs=[smem] * 3 + [vmem] * len(operands),
        out_specs=vmem,
        scratch_shapes=[pltpu.VMEM(*entry) for entry in scratch],
        compiler_params=pltpu.CompilerParams(
            vmem_limit_bytes=bytes_of(*scratch, *held) + SMALL_LIMIT
        ),
        cost_estimate=pl.CostEstimate(
            flops=8 * channels * basis_count * BLOCK * target_total,
            bytes_accessed=channels * target_total * 8,
            transcendentals=0,
        ),
        name="messages",
    )(info, lists, counts, *operands)


def mixing_kernel(info, base, ewald, gain, *refs, parts, pieces, per_device):
    total = 1 + (parts - 1) * pieces
    in_refs, out_refs = refs[:total], refs[total : 2 * total]
    out, mixed, normed, active = refs[2 * total :]
    channels, width = base.shape
    part_rows = channels // parts
    chan, first_piece = info[1], info[4]
    squares = jnp.zeros((1, width), jnp.float32)
    for part in range(parts):
        other = lax.rem(chan + part, parts)
        for start in range(0, part_rows, per_device):
            rows = pl.ds(part * part_rows + start, per_device)
            piece = ewald[(start // per_device) * parts + other].astype(jnp.float32)
            value = (base[rows] + piece).astype(jnp.bfloat16).astype(jnp.float32)
            mixed[rows] = value
            squares = squares + jnp.sum(value * value, axis=0, keepdims=True)
    factor = lax.rsqrt(squares * (1.0 / channels) + epsilon)
    for part in range(parts):
        other = lax.rem(chan + part, parts)
        rows = pl.ds(part * part_rows, part_rows)
        here = pl.ds(pl.multiple_of(other * part_rows, part_rows), part_rows)
        normed[rows] = (mixed[rows] * factor * gain[here]).astype(jnp.bfloat16)
    piece_rows = in_refs[0].shape[0] // pieces
    step = min(256, piece_rows)
    for piece in range(pieces):
        at = lax.rem(first_piece + piece, pieces) * piece_rows
        for start in range(0, piece_rows, step):
            rows = pl.ds(pl.multiple_of(at + start, step), step)
            hidden = jnp.dot(
                in_refs[0][rows], normed[0:part_rows], preferred_element_type=jnp.float32
            )
            for part in range(1, parts):
                hidden = hidden + jnp.dot(
                    in_refs[1 + (part - 1) * pieces + piece][start : start + step],
                    normed[part * part_rows : (part + 1) * part_rows],
                    preferred_element_type=jnp.float32,
                )
            active[rows] = jax.nn.gelu(hidden).astype(jnp.bfloat16)
    for part in range(parts):
        count = 1 if part == 0 else pieces
        rows = part_rows // count
        other = lax.rem(chan + part, parts) * part_rows
        for piece in range(count):
            ref = out_refs[part and 1 + (part - 1) * pieces + piece]
            value = jnp.dot(ref[...], active[...], preferred_element_type=jnp.float32)
            at = lax.rem(first_piece + piece, count) * rows
            here = pl.ds(pl.multiple_of(other + at, rows), rows)
            there = pl.ds(pl.multiple_of(part * part_rows + at, rows), rows)
            out[here] = (mixed[there] + value).astype(jnp.bfloat16)


def mixing_call(info, base, ewald, gain, ins, outs, parts, pieces):
    channels, width = base.shape
    hidden = ins[0].shape[0]
    smem = pl.BlockSpec(memory_space=pltpu.SMEM)
    vmem = pl.BlockSpec(memory_space=pltpu.VMEM)
    operands = [base, ewald, gain, *ins, *outs]
    scratch = [
        ((channels, width), jnp.float32),
        ((channels, width), jnp.bfloat16),
        ((hidden, width), jnp.bfloat16),
    ]
    held = [((channels, width), jnp.bfloat16), *((v.shape, v.dtype) for v in operands)]
    return pl.pallas_call(
        functools.partial(
            mixing_kernel, parts=parts, pieces=pieces, per_device=ewald.shape[1]
        ),
        out_shape=jax.ShapeDtypeStruct((channels, width), jnp.bfloat16),
        in_specs=[smem] + [vmem] * len(operands),
        out_specs=vmem,
        scratch_shapes=[pltpu.VMEM(*entry) for entry in scratch],
        compiler_params=pltpu.CompilerParams(
            vmem_limit_bytes=bytes_of(*scratch, *held) + SMALL_LIMIT
        ),
        cost_estimate=pl.CostEstimate(
            flops=4 * channels * hidden * width,
            bytes_accessed=4 * channels * hidden,
            transcendentals=hidden * width,
        ),
        name="mixing",
    )(info, *operands)


def chan_parts(value, count):
    return [value] + [
        lax.ppermute(value, "chan", [((i + part) % count, i) for i in range(count)])
        for part in range(1, count)
    ]


def body(
    features, positions, lists, counts, fourier_filter, radial_weights, norm_gain, mlp_in, mlp_out
):
    part_rows, atom_count = features.shape
    bricks, chans = lax.axis_size("brick"), lax.axis_size("chan")
    brick, chan = lax.axis_index("brick"), lax.axis_index("chan")
    blocks_dev = atom_count // BLOCK
    basis_count = radial_weights.shape[0]
    per_device = part_rows // bricks
    padded = -(-per_device // 16) * 16
    width = atom_count // chans
    rim = blocks_dev // 2 * BLOCK

    if per_device % 16 == 0:
        sent = pack_call(features, positions, bricks)
    else:
        sent = features.reshape(bricks, per_device, atom_count)
        sent = jnp.pad(sent, ((0, 0), (0, padded - per_device), (0, 0)))
        place_rows = split_places(positions, blocks_dev)[None]
        sent = jnp.concatenate(
            [sent, jnp.broadcast_to(place_rows, (bricks, PLACE_ROWS, atom_count))], axis=1
        )
    gathered = lax.all_to_all(sent, "brick", 0, 0)

    filters = lax.dynamic_slice_in_dim(fourier_filter, brick * per_device, per_device, 0)
    if padded != per_device:
        filters = jnp.pad(filters, ((0, padded - per_device), (0, 0)))

    owns = chan_parts(features, chans)
    gains = [value.T for value in chan_parts(radial_weights, chans)]
    head = features[:, :rim]
    tail = features[:, atom_count - rim :]
    if chans == 2 and blocks_dev == 2 * REACH:
        lower = chan == 0
        names = ("brick", "chan")

        def source(low_from, high_from):
            pairs = []
            for i in range(bricks):
                pairs.append((((i - 1) % bricks) * 2 + low_from, i * 2))
                pairs.append((((i + 1) % bricks) * 2 + high_from, i * 2 + 1))
            return pairs

        first = jnp.where(lower, tail, head)
        second = jnp.where(lower, head, tail)
        halos = [
            lax.ppermute(first, names, source(0, 1)),
            lax.ppermute(second, names, source(1, 0)),
        ]
        own_slot = jnp.where(lower, REACH, 0)
        halo_slots = [jnp.where(lower, i, blocks_dev + i) for i in range(REACH)]
        first_window = jnp.where(lower, 0, REACH)
    else:
        before = lax.ppermute(tail, "brick", [(i, (i + 1) % bricks) for i in range(bricks)])
        after = lax.ppermute(head, "brick", [((i + 1) % bricks, i) for i in range(bricks)])
        halos = chan_parts(jnp.concatenate([before, after], axis=1), chans)
        own_slot = rim // BLOCK
        halo_slots = [i for i in range(rim // BLOCK)]
        halo_slots += [rim // BLOCK + blocks_dev + i for i in range(rim // BLOCK)]
        first_window = 0
    pieces = 2 if bricks % 2 == 0 else 1
    first_piece = lax.rem(brick, pieces)
    numbers = [brick, chan, first_window, own_slot, first_piece, *halo_slots]
    info = jnp.stack([jnp.asarray(v, jnp.int32) for v in numbers])
    ins = weight_pieces(mlp_in, chans, pieces, first_piece)
    outs = weight_pieces(mlp_out, chans, pieces, first_piece)

    gathered, filters, info, gain, listed = lax.optimization_barrier(
        (gathered, filters, info, norm_gain[:, None], lists.reshape(-1))
    )
    halves = chans if width % BLOCK == 0 else 1
    ewald, near = ewald_call(info, gathered, filters, halves)
    ewald = ewald[:, :per_device]
    if halves != chans:
        ewald = ewald.reshape(bricks, per_device, chans, width)
        ewald = ewald.transpose(0, 2, 1, 3).reshape(bricks * chans, per_device, width)
    arrived = lax.all_to_all(ewald, ("brick", "chan"), 0, 0)

    ins = swap_pieces(ins, bricks, pieces)
    outs = swap_pieces(outs, bricks, pieces)
    base = message_call(
        info, listed, counts, near, positions, owns, halos, gains, basis_count
    )
    return mixing_call(info, base, arrived, gain, ins, outs, chans, pieces)


def weight_pieces(value, chans, pieces, first_piece):
    rows = value.shape[0] // pieces
    piece = lax.dynamic_slice_in_dim(value, first_piece * rows, rows, 0)
    return [value, *chan_parts(piece, chans)[1:]]


def swap_pieces(values, bricks, pieces):
    if pieces == 1:
        return values
    swapped = [values[0]]
    for value in values[1:]:
        swapped += [value, lax.ppermute(value, "brick", [(i, i ^ 1) for i in range(bricks)])]
    return swapped


def solution(mesh):
    placed = (
        P("chan", "brick"),
        P(None, "brick"),
        P("brick", None),
        P("brick"),
        P("chan", None),
        P(None, "chan"),
        P(),
        P(None, "chan"),
        P("chan", None),
    )

    return jax.shard_map(
        body, mesh=mesh, in_specs=placed, out_specs=P(None, ("brick", "chan")), check_vma=False
    )
```

```python
import functools
import math

import jax
import jax.numpy as jnp
from jax import lax
from jax.experimental import pallas as pl
from jax.experimental.pallas import tpu as pltpu
from jax.sharding import PartitionSpec as P


KSIDE = 16
BLOCK = 128
REACH = 2
brick_width = 4.0
cross_width = 8.0
cutoff = 2.0
epsilon = 1e-06

HALF = KSIDE // 2
PLANE = KSIDE * KSIDE
PLACE_ROWS = 8
LANES = 128
SMALL_LIMIT = 4 * 1024 * 1024
LARGE_LIMIT = 60 * 1024 * 1024
NT = (((1,), (1,)), ((), ()))

SIN_TERMS = (3.14159258, -5.1677069, 2.55003164, -0.59804645, 0.07722225)
COS_TERMS = (0.99999995, -4.93479286, 4.05841191, -1.33188016, 0.2196968)


def horner(terms, squared):
    value = squared * terms[-1] + terms[-2]
    for term in terms[-3::-1]:
        value = value * squared + term
    return value


def turn_cos_sin(turns):
    near = turns - jnp.round(turns)
    squared = near * near
    sine = near * horner(SIN_TERMS, squared)
    double = sine + sine
    return 1.0 - double * sine, double * horner(COS_TERMS, squared)


def same_row(ref, row, count):
    return ref[pl.ds(row, count, stride=0), :]


def read_places(ref, count):
    first = same_row(ref, 0, count) + same_row(ref, 3, count)
    second = same_row(ref, 1, count) + same_row(ref, 4, count) + same_row(ref, 6, count)
    third = same_row(ref, 2, count) + same_row(ref, 5, count) + same_row(ref, 7, count)
    return first, second, third


def split_places(positions, blocks_dev):
    atom_count = positions.shape[1]
    own_block = (jnp.arange(atom_count, dtype=jnp.int32) // BLOCK).astype(jnp.float32)
    rest = jnp.stack([positions[0] * blocks_dev - own_block, positions[1], positions[2]])
    pieces = []
    for _ in range(3):
        piece = lax.reduce_precision(rest, 8, 7)
        pieces.append(piece)
        rest = rest - piece
    pieces[2] = pieces[2][1:]
    return jnp.concatenate(pieces).astype(jnp.bfloat16)


def three_pieces(value):
    high = value.astype(jnp.bfloat16).astype(jnp.float32)
    value = value - high
    middle = value.astype(jnp.bfloat16).astype(jnp.float32)
    return high, middle, value - middle


def pack_kernel(
    features, positions, radial, sent, own, first, second, rows, whole, places, gains, sems
):
    bricks, rows_out, atom_count = sent.shape
    per_device = rows_out - PLACE_ROWS
    part_rows = bricks * per_device
    basis_count = radial.shape[0]
    rim = first.shape[1]
    copies = [
        pltpu.make_async_copy(source, target, sems.at[i])
        for i, (source, target) in enumerate(
            ((positions, places), (radial, gains), (features, whole))
        )
    ]
    for copy in copies:
        copy.start()
    blocks_dev = atom_count // BLOCK
    own_block = lax.broadcasted_iota(jnp.int32, (1, atom_count), 1) // BLOCK
    copies[0].wait()
    rows[0:1] = places[0:1] * blocks_dev - own_block.astype(jnp.float32)
    rows[1:3] = places[1:3]
    high, middle, low = three_pieces(rows[0:3])
    rows[0:3] = high
    rows[3:6] = middle
    rows[6:8] = low[1:3]
    place_rows = rows[...].astype(jnp.bfloat16)
    copies[1].wait()
    own[part_rows:] = jnp.zeros((3 * basis_count, atom_count), jnp.bfloat16)
    for i, piece in enumerate(three_pieces(gains[...])):
        at = part_rows + i * basis_count
        own[at : at + basis_count, 0:part_rows] = piece.astype(jnp.bfloat16)
    copies[2].wait()
    for device in range(bricks):
        here = slice(device * per_device, (device + 1) * per_device)
        sent[device, 0:per_device] = whole[here]
        sent[device, per_device:] = place_rows
    own[0:part_rows] = whole[...]

    lower = lax.axis_index("chan") == 0

    @pl.when(lower)
    def _():
        first[...] = whole[:, atom_count - rim :]
        second[...] = whole[:, 0:rim]

    @pl.when(jnp.logical_not(lower))
    def _():
        first[...] = whole[:, 0:rim]
        second[...] = whole[:, atom_count - rim :]


def pack_call(features, positions, radial, bricks, rim):
    part_rows, atom_count = features.shape
    per_device = part_rows // bricks
    extra = 3 * radial.shape[0]
    vmem = pl.BlockSpec(memory_space=pltpu.VMEM)
    anywhere = pl.BlockSpec(memory_space=pltpu.HBM)
    outs = [
        (bricks, per_device + PLACE_ROWS, atom_count),
        (part_rows + extra, atom_count),
        (part_rows, rim),
        (part_rows, rim),
    ]
    return pl.pallas_call(
        pack_kernel,
        out_shape=[jax.ShapeDtypeStruct(shape, jnp.bfloat16) for shape in outs],
        in_specs=[anywhere, anywhere, anywhere],
        out_specs=[vmem] * 4,
        scratch_shapes=[
            pltpu.VMEM((PLACE_ROWS, atom_count), jnp.float32),
            pltpu.VMEM(features.shape, features.dtype),
            pltpu.VMEM(positions.shape, positions.dtype),
            pltpu.VMEM(radial.shape, radial.dtype),
            pltpu.SemaphoreType.DMA((3,)),
        ],
        compiler_params=pltpu.CompilerParams(vmem_limit_bytes=LARGE_LIMIT),
        name="pack",
    )(features, positions, radial)


def pick_kernel(info, *refs):
    count = len(refs) // 2
    sources, targets, sems = refs[:count], refs[count:-1], refs[-1]
    copies = []
    for i, (source, target) in enumerate(zip(sources, targets)):
        rows = target.shape[0]
        index = info[0] if i == 0 else info[4]
        here = pl.ds(pl.multiple_of(index * rows, rows), rows)
        copies.append(pltpu.make_async_copy(source.at[here], target, sems.at[i]))
        copies[i].start()
    for copy in copies:
        copy.wait()


def pick_call(info, values, counts):
    smem, vmem = pl.BlockSpec(memory_space=pltpu.SMEM), pl.BlockSpec(memory_space=pltpu.VMEM)
    return pl.pallas_call(
        pick_kernel,
        out_shape=[
            jax.ShapeDtypeStruct((v.shape[0] // count, v.shape[1]), v.dtype)
            for v, count in zip(values, counts)
        ],
        in_specs=[smem] + [pl.BlockSpec(memory_space=pltpu.HBM)] * len(values),
        out_specs=[vmem] * len(values),
        scratch_shapes=[pltpu.SemaphoreType.DMA((len(values),))],
        compiler_params=pltpu.CompilerParams(vmem_limit_bytes=SMALL_LIMIT),
        name="pick",
    )(info, *(pltpu.with_memory_space_constraint(v, pltpu.HBM) for v in values))


def ewald_kernel(
    info,
    gathered,
    filters,
    out,
    near,
    places,
    table,
    y_table,
    depth_table,
    scaled,
    sums,
    weights,
    *,
    halves,
):
    bricks, rows_in, atom_count = gathered.shape
    channels = rows_in - PLACE_ROWS
    groups = atom_count // LANES
    total = bricks * atom_count
    blocks_dev = atom_count // BLOCK
    inverse = 1.0 / math.sqrt(total)
    lane_block = lax.broadcasted_iota(jnp.int32, (1, atom_count), 1) // BLOCK
    lane_block = lane_block.astype(jnp.float32)
    wave = lax.broadcasted_iota(jnp.int32, (HALF, 1), 0).astype(jnp.float32) + 1.0
    mid_wave = wave - 0.5

    def make_tables(brick, slot):
        places[slot] = gathered[brick, channels:, :].astype(jnp.float32)
        first, second, third = read_places(places.at[slot], HALF)
        start = (brick * blocks_dev).astype(jnp.float32) + lane_block
        along = (first + start) * (1.0 / (blocks_dev * bricks))
        centre = 0.5 * (second + third)
        low_cos, low_sin = turn_cos_sin(wave * along - centre)
        high_cos, high_sin = turn_cos_sin((wave + HALF) * along - centre)
        y_cos, y_sin = turn_cos_sin(mid_wave * second)
        z_cos, z_sin = turn_cos_sin(mid_wave * third)
        for group in range(groups):
            lanes = slice(group * LANES, (group + 1) * LANES)
            y_ref, z_ref = y_table.at[slot, group], depth_table.at[brick, group]
            y_ref[0:HALF] = y_cos[:, lanes]
            y_ref[HALF:] = y_sin[:, lanes]
            z_ref[0:HALF] = z_cos[:, lanes]
            z_ref[HALF:] = z_sin[:, lanes]
            here = brick * groups + group
            x_cos = jnp.concatenate([low_cos[:, lanes], high_cos[:, lanes]], axis=0)
            x_sin = jnp.concatenate([low_sin[:, lanes], high_sin[:, lanes]], axis=0)
            for k in range(HALF):
                cos_row = same_row(y_ref, k, KSIDE)
                sin_row = same_row(y_ref, HALF + k, KSIDE)
                a, b = x_cos * cos_row, x_sin * sin_row
                c, d = x_sin * cos_row, x_cos * sin_row
                above, below = (HALF + k) * KSIDE, (HALF - 1 - k) * KSIDE
                table[here, above : above + KSIDE] = (a - b).astype(jnp.bfloat16)
                table[here, PLANE + above : PLANE + above + KSIDE] = (c + d).astype(jnp.bfloat16)
                table[here, below : below + KSIDE] = (a + b).astype(jnp.bfloat16)
                table[here, PLANE + below : PLANE + below + KSIDE] = (c - d).astype(jnp.bfloat16)
            values = gathered[brick, 0:channels, lanes].astype(jnp.float32)
            for k in range(KSIDE):
                factor = same_row(z_ref, k, channels)
                scaled[slot, group, k * channels : (k + 1) * channels] = (values * factor).astype(
                    jnp.bfloat16
                )

    def table_of(brick):
        return jnp.concatenate([table[brick * groups + group] for group in range(groups)], axis=1)

    def add_sums(brick, slot):
        rows = jnp.concatenate([scaled[slot, group] for group in range(groups)], axis=1)
        sums[...] += lax.dot_general(rows, table_of(brick), NT, preferred_element_type=jnp.float32)

    sums[...] = jnp.zeros_like(sums)
    for step in range(3):
        neighbour = lax.rem(info[0] + (step - 1 + bricks), bricks)
        rows = gathered[neighbour, channels:, :].astype(jnp.float32)
        for block in range(blocks_dev):
            near[step * blocks_dev + block] = rows[:, block * BLOCK : (block + 1) * BLOCK]

    turn = 4
    turns = (bricks - 1) // turn
    make_tables(jnp.int32(0), 0)

    @pl.loop(0, turns)
    def _(at):
        for step in range(turn):
            add_sums(turn * at + step, step % 2)
            make_tables(turn * at + step + 1, (step + 1) % 2)

    for brick in range(turn * turns, bricks):
        add_sums(brick, brick % 2)
        if brick + 1 < bricks:
            make_tables(jnp.int32(brick + 1), (brick + 1) % 2)

    for k in range(HALF):
        upper = filters[:, pl.ds((HALF + k) * PLANE, PLANE)]
        lower = filters[:, pl.ds((HALF - 1 - k) * PLANE, PLANE)]
        both, apart = (upper + lower) * inverse, (upper - lower) * inverse
        cos_rows = pl.ds(k * channels, channels)
        sin_rows = pl.ds((HALF + k) * channels, channels)
        cos_real, cos_imag = sums[cos_rows, 0:PLANE], sums[cos_rows, PLANE:]
        sin_real, sin_imag = sums[sin_rows, 0:PLANE], sums[sin_rows, PLANE:]
        for row_part, first_part, value in (
            (cos_rows, 0, both * cos_real - apart * sin_imag),
            (cos_rows, PLANE, both * cos_imag + apart * sin_real),
            (sin_rows, 0, apart * cos_imag + both * sin_real),
            (sin_rows, PLANE, both * sin_imag - apart * cos_real),
        ):
            value = value.astype(jnp.bfloat16)
            for at in range(0, PLANE, LANES):
                weights[(first_part + at) // LANES, row_part] = value[:, at : at + LANES]

    @pl.loop(0, bricks, unroll=8)
    def _(brick):
        rows = jnp.concatenate([weights[at] for at in range(2 * PLANE // LANES)], axis=1)
        mixed = jnp.dot(rows, table_of(brick), preferred_element_type=jnp.float32)
        values = []
        for group in range(groups):
            z_ref = depth_table.at[brick, group]
            lanes = slice(group * LANES, (group + 1) * LANES)
            value = mixed[0:channels, lanes] * same_row(z_ref, 0, channels)
            for k in range(1, KSIDE):
                part = mixed[k * channels : (k + 1) * channels, lanes]
                value = value + part * same_row(z_ref, k, channels)
            values.append(value)
        value = jnp.concatenate(values, axis=1)
        value = (value * inverse).astype(jnp.bfloat16)
        width = atom_count // halves
        for part in range(halves):
            out[brick * halves + part] = value[:, part * width : (part + 1) * width]


def bytes_of(*shapes):
    total = 0
    for shape, dtype in shapes:
        padded = [*shape[:-2], -(-shape[-2] // 16) * 16, -(-shape[-1] // LANES) * LANES]
        total += math.prod(padded) * jnp.dtype(dtype).itemsize
    return total


def ewald_call(info, gathered, filters, halves):
    bricks, rows_in, atom_count = gathered.shape
    channels = rows_in - PLACE_ROWS
    total = bricks * atom_count
    rows = KSIDE * channels
    scratch = [
        ((2, PLACE_ROWS, atom_count), jnp.float32),
        ((total // LANES, 2 * PLANE, LANES), jnp.bfloat16),
        ((2, atom_count // LANES, KSIDE, LANES), jnp.float32),
        ((bricks, atom_count // LANES, KSIDE, LANES), jnp.float32),
        ((2, atom_count // LANES, rows, LANES), jnp.bfloat16),
        ((rows, 2 * PLANE), jnp.float32),
        ((2 * PLANE // LANES, rows, LANES), jnp.bfloat16),
    ]
    out = ((bricks * halves, channels, atom_count // halves), jnp.bfloat16)
    near = ((3 * atom_count // BLOCK, PLACE_ROWS, BLOCK), jnp.float32)
    held = [out, near, (gathered.shape, gathered.dtype), (filters.shape, filters.dtype)]
    smem, vmem = pl.BlockSpec(memory_space=pltpu.SMEM), pl.BlockSpec(memory_space=pltpu.VMEM)
    return pl.pallas_call(
        functools.partial(ewald_kernel, halves=halves),
        out_shape=(jax.ShapeDtypeStruct(*out), jax.ShapeDtypeStruct(*near)),
        in_specs=[smem, vmem, vmem],
        out_specs=(vmem, vmem),
        scratch_shapes=[pltpu.VMEM(*entry) for entry in scratch],
        compiler_params=pltpu.CompilerParams(
            vmem_limit_bytes=bytes_of(*scratch, *held) + SMALL_LIMIT
        ),
        cost_estimate=pl.CostEstimate(
            flops=8 * rows * PLANE * total,
            bytes_accessed=gathered.size * 2 + filters.size * 4,
            transcendentals=0,
        ),
        name="ewald",
    )(info, gathered, filters)


def message_kernel(info, lists, counts, near, positions, *refs, parts, basis_count):
    sources = refs[: 2 * parts]
    out, *buffers, scaled, gains, running, sems = refs[2 * parts :]
    copies = [
        pltpu.make_async_copy(source, buffer, sems.at[i])
        for i, (source, buffer) in enumerate(zip(sources, buffers))
    ]
    for copy in copies:
        copy.start()
    own_refs, halo_refs = buffers[:parts], buffers[parts:]
    atom_count = own_refs[0].shape[1]
    part_rows = own_refs[0].shape[0] - 3 * basis_count
    own_blocks = atom_count // BLOCK
    halo_blocks = halo_refs[0].shape[1] // BLOCK
    channels, target_total = out.shape
    tile = min(BLOCK, target_total)
    spacing = cutoff / (basis_count - 1)
    root = math.sqrt(math.log2(math.e))
    chan, first_window, own_slot = info[1], info[2], info[3]
    step = 16

    for part in range(parts):
        copies[part].wait()
        copies[parts + part].wait()
        for at in range(0, part_rows, LANES):
            rows = [
                own_refs[part][
                    part_rows + i * basis_count : part_rows + (i + 1) * basis_count,
                    at : at + LANES,
                ].astype(jnp.float32)
                for i in range(3)
            ]
            count = min(LANES, part_rows - at)
            turned = (rows[0] + rows[1] + rows[2]).T
            gains[part * part_rows + at : part * part_rows + at + count] = turned[0:count]

        @pl.loop(0, part_rows // step, unroll=2)
        def _(group):
            rows = pl.ds(pl.multiple_of(group * step, step), step)
            into = pl.ds(pl.multiple_of(part * part_rows + group * step, step), step)
            columns = gains[into]
            factors = [
                jnp.broadcast_to(columns[:, m : m + 1], (step, BLOCK)) for m in range(basis_count)
            ]
            blocks = [(own_refs[part], i, own_slot + i) for i in range(own_blocks)]
            blocks += [(halo_refs[part], i, info[5 + i]) for i in range(halo_blocks)]
            for ref, block, slot in blocks:
                value = ref[rows, block * BLOCK : (block + 1) * BLOCK].astype(jnp.float32)
                for m in range(basis_count):
                    scaled[slot, m, into] = (value * factors[m]).astype(jnp.bfloat16)

    first_target = chan * target_total
    tiles = range(target_total // tile)
    target_blocks = [(first_target + i * tile) // BLOCK for i in tiles]
    target_places = []
    for i in tiles:
        running[i] = jnp.zeros((tile, channels), jnp.float32)
        places = own_tile(positions, first_target, i * tile, tile)
        places = jnp.concatenate([places, jnp.zeros((8 - 3, tile), jnp.float32)]).T
        target_places.append(
            [
                jnp.broadcast_to(places[:, axis : axis + 1] * scale, (tile, BLOCK))
                for axis, scale in enumerate((brick_width, cross_width, cross_width))
            ]
        )

    def add_entry(i, entry):
        x_target, y_target, z_target = target_places[i]
        used = entry < counts[target_blocks[i]]
        listed = lists[target_blocks[i], entry]
        first, second, third = read_places(near.at[listed + (own_blocks - REACH)], 8)
        first = (first + (listed - REACH).astype(jnp.float32)) * (brick_width / own_blocks)
        second, third = second * cross_width, third * cross_width
        dx = jnp.concatenate([first] * (tile // 8)) - x_target
        dy = jnp.concatenate([second] * (tile // 8)) - y_target
        dz = jnp.concatenate([third] * (tile // 8)) - z_target
        squared = dx * dx + dy * dy + dz * dz
        reach = jnp.sqrt(squared) * (root / spacing)
        envelope = jnp.maximum(1.0 - squared * (1.0 / (cutoff * cutoff)), 0.0)
        envelope = envelope * envelope * used.astype(jnp.float32)
        basis = []
        for m in range(basis_count):
            gap = reach - m * root
            basis.append((jnp.exp2(-(gap * gap)) * envelope).astype(jnp.bfloat16))
        source = scaled.at[listed - first_window]
        running[i] += lax.dot_general(
            jnp.concatenate(basis, axis=1),
            jnp.concatenate([source[m] for m in range(basis_count)], axis=1),
            NT,
            preferred_element_type=jnp.float32,
        )

    longest = counts[target_blocks[0]]
    for block in target_blocks[1:]:
        longest = jnp.maximum(longest, counts[block])

    @pl.loop(0, longest)
    def _(entry):
        for i in tiles:
            add_entry(i, entry)

    for i in tiles:
        summed = running[i].T
        for part in range(parts):
            own = own_tile(own_refs[part].at[0:part_rows], first_target, i * tile, tile)
            out[pl.ds(part * part_rows, part_rows), i * tile : (i + 1) * tile] = (
                own.astype(jnp.float32) + summed[part * part_rows : (part + 1) * part_rows]
            )


def own_tile(ref, first, start, width):
    if width % LANES == 0:
        return ref[:, pl.ds(pl.multiple_of(first + start, LANES), width)]
    value = ref[...]
    picked = value[:, 0:width]
    for at in range(width, value.shape[1], width):
        picked = jnp.where(first + start == at, value[:, at : at + width], picked)
    return picked


def message_call(info, lists, counts, near, positions, owns, halos, basis_count):
    parts = len(owns)
    own_rows, atom_count = owns[0].shape
    channels = parts * (own_rows - 3 * basis_count)
    slots = (atom_count + halos[0].shape[1]) // BLOCK
    target_total = atom_count // parts
    tile = min(BLOCK, target_total)
    smem, vmem = pl.BlockSpec(memory_space=pltpu.SMEM), pl.BlockSpec(memory_space=pltpu.VMEM)
    moved = [*owns, *halos]
    scratch = [(value.shape, value.dtype) for value in moved] + [
        ((slots, basis_count, channels, BLOCK), jnp.bfloat16),
        ((channels, basis_count), jnp.float32),
        ((target_total // tile, tile, channels), jnp.float32),
    ]
    out = ((channels, target_total), jnp.float32)
    held = [out, (near.shape, near.dtype), (positions.shape, positions.dtype)]
    return pl.pallas_call(
        functools.partial(message_kernel, parts=parts, basis_count=basis_count),
        out_shape=jax.ShapeDtypeStruct(*out),
        in_specs=[smem] * 3 + [vmem] * 2 + [pl.BlockSpec(memory_space=pltpu.HBM)] * len(moved),
        out_specs=vmem,
        scratch_shapes=[pltpu.VMEM(*entry) for entry in scratch]
        + [pltpu.SemaphoreType.DMA((len(moved),))],
        compiler_params=pltpu.CompilerParams(
            vmem_limit_bytes=bytes_of(*scratch, *held) + SMALL_LIMIT
        ),
        cost_estimate=pl.CostEstimate(
            flops=8 * channels * basis_count * BLOCK * target_total,
            bytes_accessed=channels * target_total * 8,
            transcendentals=0,
        ),
        name="messages",
    )(
        info,
        lists,
        counts,
        near,
        positions,
        *(pltpu.with_memory_space_constraint(value, pltpu.HBM) for value in moved),
    )


def mixing_kernel(info, base, ewald, gain, *refs, parts, pieces, per_device):
    total = 1 + (parts - 1) * pieces
    in_refs, out_refs = refs[:total], refs[total : 2 * total]
    out, mixed, normed, active, gains = refs[2 * total :]
    channels, width = base.shape
    part_rows = channels // parts
    chan, first_piece = info[1], info[4]
    for at in range(0, channels, LANES):
        gains[at : at + LANES] = jnp.broadcast_to(gain[:, at : at + LANES], (8, LANES)).T
    squares = jnp.zeros((1, width), jnp.float32)
    for part in range(parts):
        other = lax.rem(chan + part, parts)
        for start in range(0, part_rows, per_device):
            rows = pl.ds(part * part_rows + start, per_device)
            piece = ewald[(start // per_device) * parts + other].astype(jnp.float32)
            value = (base[rows] + piece).astype(jnp.bfloat16).astype(jnp.float32)
            mixed[rows] = value
            squares = squares + jnp.sum(value * value, axis=0, keepdims=True)
    factor = lax.rsqrt(squares * (1.0 / channels) + epsilon)
    for part in range(parts):
        other = lax.rem(chan + part, parts)
        rows = pl.ds(part * part_rows, part_rows)
        here = pl.ds(pl.multiple_of(other * part_rows, part_rows), part_rows)
        normed[rows] = (mixed[rows] * factor * gains[here, 0:1]).astype(jnp.bfloat16)
    piece_rows = in_refs[0].shape[0] // pieces
    step = min(256, piece_rows)
    for piece in range(pieces):
        at = lax.rem(first_piece + piece, pieces) * piece_rows
        for start in range(0, piece_rows, step):
            rows = pl.ds(pl.multiple_of(at + start, step), step)
            hidden = jnp.dot(
                in_refs[0][rows], normed[0:part_rows], preferred_element_type=jnp.float32
            )
            for part in range(1, parts):
                hidden = hidden + jnp.dot(
                    in_refs[1 + (part - 1) * pieces + piece][start : start + step],
                    normed[part * part_rows : (part + 1) * part_rows],
                    preferred_element_type=jnp.float32,
                )
            active[rows] = jax.nn.gelu(hidden).astype(jnp.bfloat16)
    for part in range(parts):
        count = 1 if part == 0 else pieces
        rows = part_rows // count
        other = lax.rem(chan + part, parts) * part_rows
        for piece in range(count):
            ref = out_refs[part and 1 + (part - 1) * pieces + piece]
            value = jnp.dot(ref[...], active[...], preferred_element_type=jnp.float32)
            at = lax.rem(first_piece + piece, count) * rows
            here = pl.ds(pl.multiple_of(other + at, rows), rows)
            there = pl.ds(pl.multiple_of(part * part_rows + at, rows), rows)
            out[here] = (mixed[there] + value).astype(jnp.bfloat16)


def mixing_call(info, base, ewald, gain, ins, outs, parts, pieces):
    channels, width = base.shape
    hidden = ins[0].shape[0]
    smem = pl.BlockSpec(memory_space=pltpu.SMEM)
    vmem = pl.BlockSpec(memory_space=pltpu.VMEM)
    operands = [base, ewald, gain, *ins, *outs]
    scratch = [
        ((channels, width), jnp.float32),
        ((channels, width), jnp.bfloat16),
        ((hidden, width), jnp.bfloat16),
        ((channels, 8), jnp.float32),
    ]
    held = [((channels, width), jnp.bfloat16), *((v.shape, v.dtype) for v in operands)]
    return pl.pallas_call(
        functools.partial(
            mixing_kernel, parts=parts, pieces=pieces, per_device=ewald.shape[1]
        ),
        out_shape=jax.ShapeDtypeStruct((channels, width), jnp.bfloat16),
        in_specs=[smem] + [vmem] * len(operands),
        out_specs=vmem,
        scratch_shapes=[pltpu.VMEM(*entry) for entry in scratch],
        compiler_params=pltpu.CompilerParams(
            vmem_limit_bytes=bytes_of(*scratch, *held) + SMALL_LIMIT
        ),
        cost_estimate=pl.CostEstimate(
            flops=4 * channels * hidden * width,
            bytes_accessed=4 * channels * hidden,
            transcendentals=hidden * width,
        ),
        name="mixing",
    )(info, *operands)


def chan_parts(value, count):
    return [value] + [
        lax.ppermute(value, "chan", [((i + part) % count, i) for i in range(count)])
        for part in range(1, count)
    ]


def body(
    features, positions, lists, counts, fourier_filter, radial_weights, norm_gain, mlp_in, mlp_out
):
    part_rows, atom_count = features.shape
    bricks, chans = lax.axis_size("brick"), lax.axis_size("chan")
    brick, chan = lax.axis_index("brick"), lax.axis_index("chan")
    blocks_dev = atom_count // BLOCK
    basis_count = radial_weights.shape[0]
    per_device = part_rows // bricks
    padded = -(-per_device // 16) * 16
    width = atom_count // chans
    rim = blocks_dev // 2 * BLOCK

    pieces = 2 if bricks % 2 == 0 else 1
    first_piece = lax.rem(brick, pieces)
    halved = chans == 2 and blocks_dev == 2 * REACH
    if halved:
        lower = chan == 0
        own_slot = jnp.where(lower, REACH, 0)
        halo_slots = [jnp.where(lower, i, blocks_dev + i) for i in range(REACH)]
        first_window = jnp.where(lower, 0, REACH)
    else:
        own_slot = rim // BLOCK
        halo_slots = [i for i in range(rim // BLOCK)]
        halo_slots += [rim // BLOCK + blocks_dev + i for i in range(rim // BLOCK)]
        first_window = 0
    numbers = [brick, chan, first_window, own_slot, first_piece, *halo_slots]
    info = jnp.stack([jnp.asarray(v, jnp.int32) for v in numbers])

    if halved and per_device % 16 == 0:
        sent, own, first, second = pack_call(
            features, positions, radial_weights, bricks, rim
        )
    else:
        sent = features.reshape(bricks, per_device, atom_count)
        sent = jnp.pad(sent, ((0, 0), (0, padded - per_device), (0, 0)))
        place_rows = split_places(positions, blocks_dev)[None]
        sent = jnp.concatenate(
            [sent, jnp.broadcast_to(place_rows, (bricks, PLACE_ROWS, atom_count))], axis=1
        )
        rest, radial = radial_weights, []
        for _ in range(3):
            radial.append(lax.reduce_precision(rest, 8, 7))
            rest = rest - radial[-1]
        radial = jnp.concatenate(radial).astype(jnp.bfloat16)
        radial = jnp.pad(radial, ((0, 0), (0, atom_count - part_rows)))
        own = jnp.concatenate([features, radial])
        first, second = features[:, atom_count - rim :], features[:, :rim]
        if halved:
            first, second = jnp.where(lower, first, second), jnp.where(lower, second, first)
    gathered = lax.all_to_all(sent, "brick", 0, 0)

    owns = chan_parts(own, chans)
    if halved:
        names = ("brick", "chan")

        def source(low_from, high_from):
            pairs = []
            for i in range(bricks):
                pairs.append((((i - 1) % bricks) * 2 + low_from, i * 2))
                pairs.append((((i + 1) % bricks) * 2 + high_from, i * 2 + 1))
            return pairs

        halos = [
            lax.ppermute(first, names, source(0, 1)),
            lax.ppermute(second, names, source(1, 0)),
        ]
    else:
        before = lax.ppermute(first, "brick", [(i, (i + 1) % bricks) for i in range(bricks)])
        after = lax.ppermute(second, "brick", [((i + 1) % bricks, i) for i in range(bricks)])
        halos = chan_parts(jnp.concatenate([before, after], axis=1), chans)

    if padded == per_device:
        filters, fetched_in, fetched_out = pick_call(
            info, (fourier_filter, mlp_in, mlp_out), (bricks, pieces, pieces)
        )
    else:
        filters = lax.dynamic_slice_in_dim(fourier_filter, brick * per_device, per_device, 0)
        filters = jnp.pad(filters, ((0, padded - per_device), (0, 0)))
        fetched_in, fetched_out = (
            lax.dynamic_slice_in_dim(
                value, first_piece * (value.shape[0] // pieces), value.shape[0] // pieces, 0
            )
            for value in (mlp_in, mlp_out)
        )
    ins = [mlp_in, *chan_parts(fetched_in, chans)[1:]]
    outs = [mlp_out, *chan_parts(fetched_out, chans)[1:]]

    halves = chans if width % BLOCK == 0 else 1
    ewald, near = ewald_call(info, gathered, filters, halves)
    ewald = ewald[:, :per_device]
    if halves != chans:
        ewald = ewald.reshape(bricks, per_device, chans, width)
        ewald = ewald.transpose(0, 2, 1, 3).reshape(bricks * chans, per_device, width)
    arrived = lax.all_to_all(ewald, ("brick", "chan"), 0, 0)

    ins = swap_pieces(ins, bricks, pieces)
    outs = swap_pieces(outs, bricks, pieces)
    base = message_call(
        info, lists, counts, near, positions, owns, halos, basis_count
    )
    return mixing_call(info, base, arrived, norm_gain[None, :], ins, outs, chans, pieces)


def swap_pieces(values, bricks, pieces):
    if pieces == 1:
        return values
    swapped = [values[0]]
    for value in values[1:]:
        swapped += [value, lax.ppermute(value, "brick", [(i, i ^ 1) for i in range(bricks)])]
    return swapped


def solution(mesh):
    placed = (
        P("chan", "brick"),
        P(None, "brick"),
        P("brick", None),
        P("brick"),
        P("chan", None),
        P(None, "chan"),
        P(),
        P(None, "chan"),
        P("chan", None),
    )

    return jax.shard_map(
        body, mesh=mesh, in_specs=placed, out_specs=P(None, ("brick", "chan")), check_vma=False
    )
```

```python
import functools
import math

import jax
import jax.numpy as jnp
from jax import lax
from jax.experimental import pallas as pl
from jax.experimental.pallas import tpu as pltpu
from jax.sharding import PartitionSpec as P


KSIDE = 16
BLOCK = 128
REACH = 2
brick_width = 4.0
cross_width = 8.0
cutoff = 2.0
epsilon = 1e-06

HALF = KSIDE // 2
PLANE = KSIDE * KSIDE
GELU_SCALE = math.sqrt(2.0 / math.pi)
PIECES = 2
PLACE_ROWS = 3 * PIECES
LANES = 128
SMALL_LIMIT = 4 * 1024 * 1024
LARGE_LIMIT = 60 * 1024 * 1024
NT = (((1,), (1,)), ((), ()))

SIN_TERMS = (3.14159258, -5.1677069, 2.55003164, -0.59804645, 0.07722225)
COS_TERMS = (0.99999995, -4.93479286, 4.05841191, -1.33188016, 0.2196968)


def horner(terms, squared):
    value = squared * terms[-1] + terms[-2]
    for term in terms[-3::-1]:
        value = value * squared + term
    return value


def turn_cos_sin(turns):
    near = turns - jnp.round(turns)
    squared = near * near
    sine = near * horner(SIN_TERMS, squared)
    double = sine + sine
    return 1.0 - double * sine, double * horner(COS_TERMS, squared)


def same_row(ref, row, count):
    return ref[pl.ds(row, count, stride=0), :]


def read_places(ref, group, groups, count):
    values = []
    for axis in range(3):
        pieces = [
            same_row(ref, (piece * 3 + axis) * groups + group, count) for piece in range(PIECES)
        ]
        values.append(sum(pieces[1:], pieces[0]))
    return values


def to_groups(value):
    groups = value.shape[-1] // LANES
    value = value.reshape(*value.shape[:-1], groups, LANES)
    value = jnp.swapaxes(value, -2, -3)
    return value.reshape(*value.shape[:-3], -1, LANES)


def split_places(positions, blocks_dev):
    atom_count = positions.shape[1]
    own_block = (jnp.arange(atom_count, dtype=jnp.int32) // BLOCK).astype(jnp.float32)
    rest = jnp.stack([positions[0] * blocks_dev - own_block, positions[1], positions[2]])
    pieces = []
    for _ in range(PIECES):
        pieces.append(lax.reduce_precision(rest, 8, 7))
        rest = rest - pieces[-1]
    return jnp.concatenate(pieces).astype(jnp.bfloat16).reshape(-1, LANES)


def three_pieces(value):
    high = value.astype(jnp.bfloat16).astype(jnp.float32)
    value = value - high
    middle = value.astype(jnp.bfloat16).astype(jnp.float32)
    return high, middle, value - middle


def pack_kernel(features, positions, sent, places, whole, rows, sems):
    bricks, _, _ = sent.shape
    part_rows, atom_count = features.shape
    per_device = part_rows // bricks
    groups = atom_count // LANES
    copies = [
        pltpu.make_async_copy(positions, places, sems.at[0]),
        pltpu.make_async_copy(features, whole, sems.at[1]),
    ]
    for copy in copies:
        copy.start()
    blocks_dev = atom_count // BLOCK
    own_block = lax.broadcasted_iota(jnp.int32, (1, atom_count), 1) // BLOCK
    copies[0].wait()
    places[0:1] = places[0:1] * blocks_dev - own_block.astype(jnp.float32)
    rest = places[...]
    for piece in range(PIECES):
        high = rest.astype(jnp.bfloat16).astype(jnp.float32)
        rest = rest - high
        for axis in range(3):
            for group in range(groups):
                at = (piece * 3 + axis) * groups + group
                rows[at : at + 1] = high[axis : axis + 1, group * LANES : (group + 1) * LANES]
    place_rows = rows[...].astype(jnp.bfloat16)
    copies[1].wait()
    for device in range(bricks):
        here = slice(device * per_device, (device + 1) * per_device)
        for group in range(groups):
            sent[device, group * per_device : (group + 1) * per_device] = whole[
                here, group * LANES : (group + 1) * LANES
            ]
        sent[device, groups * per_device :] = place_rows


def pack_call(features, positions, bricks):
    part_rows, atom_count = features.shape
    rows = (part_rows // bricks + PLACE_ROWS) * (atom_count // LANES)
    return pl.pallas_call(
        pack_kernel,
        out_shape=jax.ShapeDtypeStruct((bricks, rows, LANES), jnp.bfloat16),
        in_specs=[pl.BlockSpec(memory_space=pltpu.HBM)] * 2,
        out_specs=pl.BlockSpec(memory_space=pltpu.VMEM),
        scratch_shapes=[
            pltpu.VMEM(positions.shape, positions.dtype),
            pltpu.VMEM(features.shape, features.dtype),
            pltpu.VMEM((PLACE_ROWS * (atom_count // LANES), LANES), jnp.float32),
            pltpu.SemaphoreType.DMA((2,)),
        ],
        compiler_params=pltpu.CompilerParams(vmem_limit_bytes=SMALL_LIMIT),
        name="pack",
    )(*(pltpu.with_memory_space_constraint(v, pltpu.HBM) for v in (features, positions)))


def border_kernel(features, radial, own, first, second, whole, gains, sems):
    part_rows, atom_count = features.shape
    basis_count = radial.shape[0]
    rim = first.shape[1]
    copies = [
        pltpu.make_async_copy(radial, gains, sems.at[0]),
        pltpu.make_async_copy(features, whole, sems.at[1]),
    ]
    for copy in copies:
        copy.start()
    copies[0].wait()
    own[part_rows:] = jnp.zeros((3 * basis_count, atom_count), jnp.bfloat16)
    for i, piece in enumerate(three_pieces(gains[...])):
        at = part_rows + i * basis_count
        own[at : at + basis_count, 0:part_rows] = piece.astype(jnp.bfloat16)
    copies[1].wait()
    own[0:part_rows] = whole[...]
    lower = lax.axis_index("chan") == 0

    @pl.when(lower)
    def _():
        first[...] = whole[:, atom_count - rim :]
        second[...] = whole[:, 0:rim]

    @pl.when(jnp.logical_not(lower))
    def _():
        first[...] = whole[:, 0:rim]
        second[...] = whole[:, atom_count - rim :]


def border_call(features, radial, rim):
    part_rows, atom_count = features.shape
    vmem = pl.BlockSpec(memory_space=pltpu.VMEM)
    outs = [(part_rows + 3 * radial.shape[0], atom_count), (part_rows, rim), (part_rows, rim)]
    return pl.pallas_call(
        border_kernel,
        out_shape=[jax.ShapeDtypeStruct(shape, jnp.bfloat16) for shape in outs],
        in_specs=[pl.BlockSpec(memory_space=pltpu.HBM)] * 2,
        out_specs=[vmem] * 3,
        scratch_shapes=[
            pltpu.VMEM(features.shape, features.dtype),
            pltpu.VMEM(radial.shape, radial.dtype),
            pltpu.SemaphoreType.DMA((2,)),
        ],
        compiler_params=pltpu.CompilerParams(vmem_limit_bytes=LARGE_LIMIT),
        name="border",
    )(features, radial)


def pick_kernel(info, *refs):
    count = len(refs) // 2
    sources, targets, sems = refs[:count], refs[count:-1], refs[-1]
    copies = []
    for i, (source, target) in enumerate(zip(sources, targets)):
        rows = target.shape[0]
        index = info[0] if i == 0 else info[4]
        here = pl.ds(pl.multiple_of(index * rows, rows), rows)
        copies.append(pltpu.make_async_copy(source.at[here], target, sems.at[i]))
        copies[i].start()
    for copy in copies:
        copy.wait()


def pick_call(info, values, counts):
    smem, vmem = pl.BlockSpec(memory_space=pltpu.SMEM), pl.BlockSpec(memory_space=pltpu.VMEM)
    return pl.pallas_call(
        pick_kernel,
        out_shape=[
            jax.ShapeDtypeStruct((v.shape[0] // count, v.shape[1]), v.dtype)
            for v, count in zip(values, counts)
        ],
        in_specs=[smem] + [pl.BlockSpec(memory_space=pltpu.HBM)] * len(values),
        out_specs=[vmem] * len(values),
        scratch_shapes=[pltpu.SemaphoreType.DMA((len(values),))],
        compiler_params=pltpu.CompilerParams(vmem_limit_bytes=SMALL_LIMIT),
        name="pick",
    )(info, *(pltpu.with_memory_space_constraint(v, pltpu.HBM) for v in values))


def ewald_kernel(
    info,
    gathered,
    filters,
    out,
    near,
    places,
    steps,
    table,
    depth_table,
    scaled,
    sums,
    weights,
    *,
    halves,
):
    bricks, channels, atom_count = out.shape[0] // halves, out.shape[1], out.shape[2] * halves
    groups = atom_count // LANES
    total = bricks * atom_count
    blocks_dev = atom_count // BLOCK
    inverse = 1.0 / math.sqrt(total)
    row = lax.broadcasted_iota(jnp.int32, (HALF, 1), 0)
    wave = row.astype(jnp.float32) + 1.0
    quarter = HALF // 2
    upper_rows = row >= quarter
    mid_wave = lax.rem(row, quarter).astype(jnp.float32) + 0.5

    def depth_row(ref, k, sine):
        at = (k // quarter) * 4 * quarter + sine * 2 * quarter + quarter + k % quarter
        return same_row(ref, at, channels)

    def make_tables(brick, slot):
        places[slot] = gathered[brick, channels * groups :].astype(jnp.float32)
        alongs = []
        for group in range(groups):
            first, second, third = read_places(places.at[slot], group, groups, HALF)
            start = brick * blocks_dev + group * LANES // BLOCK
            along = (first + start.astype(jnp.float32)) * (1.0 / (blocks_dev * bricks))
            alongs.append((along, second, third))
            for i, turns in enumerate((HALF * along, quarter * second, quarter * third)):
                at = i * groups + group
                steps[slot, 0, at : at + 1] = turns[0:1]
        steps[slot, 0], steps[slot, 1] = turn_cos_sin(steps[slot, 0])
        step_cos, step_sin = steps.at[slot, 0], steps.at[slot, 1]
        for group in range(groups):
            along, second, third = alongs[group]
            here = brick * groups + group
            rows = depth_table.at[here]
            low_cos, low_sin = turn_cos_sin(mid_wave * jnp.where(upper_rows, third, second))
            by_cos, by_sin = (
                jnp.where(
                    upper_rows,
                    same_row(ref, 2 * groups + group, HALF),
                    same_row(ref, groups + group, HALF),
                )
                for ref in (step_cos, step_sin)
            )
            rows[0:HALF], rows[HALF : 2 * HALF] = low_cos, low_sin
            rows[2 * HALF : 3 * HALF] = low_cos * by_cos - low_sin * by_sin
            rows[3 * HALF :] = low_cos * by_sin + low_sin * by_cos

            low_cos, low_sin = turn_cos_sin(wave * along - 0.5 * (second + third))
            by_cos, by_sin = same_row(step_cos, group, HALF), same_row(step_sin, group, HALF)
            x_cos = jnp.concatenate([low_cos, low_cos * by_cos - low_sin * by_sin], axis=0)
            x_sin = jnp.concatenate([low_sin, low_cos * by_sin + low_sin * by_cos], axis=0)
            for k in range(HALF):
                at = (k // quarter) * 2 * HALF + k % quarter
                cos_row, sin_row = same_row(rows, at, KSIDE), same_row(rows, at + HALF, KSIDE)
                a, b = x_cos * cos_row, x_sin * sin_row
                c, d = x_sin * cos_row, x_cos * sin_row
                above, below = (HALF + k) * KSIDE, (HALF - 1 - k) * KSIDE
                table[here, above : above + KSIDE] = (a - b).astype(jnp.bfloat16)
                table[here, PLANE + above : PLANE + above + KSIDE] = (c + d).astype(jnp.bfloat16)
                table[here, below : below + KSIDE] = (a + b).astype(jnp.bfloat16)
                table[here, PLANE + below : PLANE + below + KSIDE] = (c - d).astype(jnp.bfloat16)
            values = gathered[brick, group * channels : (group + 1) * channels].astype(jnp.float32)
            for k in range(KSIDE):
                factor = depth_row(rows, k % HALF, k // HALF)
                scaled[slot, group, k * channels : (k + 1) * channels] = (values * factor).astype(
                    jnp.bfloat16
                )

    def table_of(brick):
        return jnp.concatenate([table[brick * groups + group] for group in range(groups)], axis=1)

    def add_sums(brick, slot):
        rows = jnp.concatenate([scaled[slot, group] for group in range(groups)], axis=1)
        sums[...] += lax.dot_general(rows, table_of(brick), NT, preferred_element_type=jnp.float32)

    sums[...] = jnp.zeros_like(sums)
    for step in range(3):
        neighbour = lax.rem(info[0] + (step - 1 + bricks), bricks)
        near[step] = gathered[neighbour, channels * groups :].astype(jnp.float32)

    turn = 4
    turns = (bricks - 1) // turn
    make_tables(jnp.int32(0), 0)

    @pl.loop(0, turns)
    def _(at):
        for step in range(turn):
            add_sums(turn * at + step, step % 2)
            make_tables(turn * at + step + 1, (step + 1) % 2)

    for brick in range(turn * turns, bricks):
        add_sums(brick, brick % 2)
        if brick + 1 < bricks:
            make_tables(jnp.int32(brick + 1), (brick + 1) % 2)

    for k in range(HALF):
        upper = filters[:, pl.ds((HALF + k) * PLANE, PLANE)]
        lower = filters[:, pl.ds((HALF - 1 - k) * PLANE, PLANE)]
        both, apart = (upper + lower) * inverse, (upper - lower) * inverse
        cos_rows = pl.ds(k * channels, channels)
        sin_rows = pl.ds((HALF + k) * channels, channels)
        cos_real, cos_imag = sums[cos_rows, 0:PLANE], sums[cos_rows, PLANE:]
        sin_real, sin_imag = sums[sin_rows, 0:PLANE], sums[sin_rows, PLANE:]
        for row_part, first_part, value in (
            (cos_rows, 0, both * cos_real - apart * sin_imag),
            (cos_rows, PLANE, both * cos_imag + apart * sin_real),
            (sin_rows, 0, apart * cos_imag + both * sin_real),
            (sin_rows, PLANE, both * sin_imag - apart * cos_real),
        ):
            value = value.astype(jnp.bfloat16)
            for at in range(0, PLANE, LANES):
                weights[(first_part + at) // LANES, row_part] = value[:, at : at + LANES]

    @pl.loop(0, bricks, unroll=8)
    def _(brick):
        coefficients = jnp.concatenate(
            [weights[at] for at in range(2 * PLANE // LANES)], axis=1
        )
        mixed = jnp.dot(coefficients, table_of(brick), preferred_element_type=jnp.float32)
        values = []
        for group in range(groups):
            rows = depth_table.at[brick * groups + group]
            lanes = slice(group * LANES, (group + 1) * LANES)
            value = mixed[0:channels, lanes] * depth_row(rows, 0, 0)
            for k in range(1, KSIDE):
                part = mixed[k * channels : (k + 1) * channels, lanes]
                value = value + part * depth_row(rows, k % HALF, k // HALF)
            values.append(value)
        value = jnp.concatenate(values, axis=1)
        value = (value * inverse).astype(jnp.bfloat16)
        width = atom_count // halves
        for part in range(halves):
            out[brick * halves + part] = value[:, part * width : (part + 1) * width]


def bytes_of(*shapes):
    total = 0
    for shape, dtype in shapes:
        padded = [*shape[:-2], -(-shape[-2] // 16) * 16, -(-shape[-1] // LANES) * LANES]
        total += math.prod(padded) * jnp.dtype(dtype).itemsize
    return total


def ewald_call(info, gathered, filters, halves):
    bricks, channels = gathered.shape[0], filters.shape[0]
    groups = gathered.shape[1] // (channels + PLACE_ROWS)
    atom_count = groups * LANES
    total = bricks * atom_count
    rows = KSIDE * channels
    scratch = [
        ((2, PLACE_ROWS * groups, LANES), jnp.float32),
        ((2, 2, 3 * groups, LANES), jnp.float32),
        ((total // LANES, 2 * PLANE, LANES), jnp.bfloat16),
        ((total // LANES, 2 * KSIDE, LANES), jnp.float32),
        ((2, atom_count // LANES, rows, LANES), jnp.bfloat16),
        ((rows, 2 * PLANE), jnp.float32),
        ((2 * PLANE // LANES, rows, LANES), jnp.bfloat16),
    ]
    out = ((bricks * halves, channels, atom_count // halves), jnp.bfloat16)
    near = ((3, PLACE_ROWS * groups, LANES), jnp.float32)
    held = [out, near, (gathered.shape, gathered.dtype), (filters.shape, filters.dtype)]
    smem, vmem = pl.BlockSpec(memory_space=pltpu.SMEM), pl.BlockSpec(memory_space=pltpu.VMEM)
    return pl.pallas_call(
        functools.partial(ewald_kernel, halves=halves),
        out_shape=(jax.ShapeDtypeStruct(*out), jax.ShapeDtypeStruct(*near)),
        in_specs=[smem, vmem, vmem],
        out_specs=(vmem, vmem),
        scratch_shapes=[pltpu.VMEM(*entry) for entry in scratch],
        compiler_params=pltpu.CompilerParams(
            vmem_limit_bytes=bytes_of(*scratch, *held) + SMALL_LIMIT
        ),
        cost_estimate=pl.CostEstimate(
            flops=8 * rows * PLANE * total,
            bytes_accessed=gathered.size * 2 + filters.size * 4,
            transcendentals=0,
        ),
        name="ewald",
    )(info, gathered, filters)


def message_kernel(info, lists, counts, near, positions, *refs, parts, basis_count):
    sources = refs[: 2 * parts]
    out, *buffers, scaled, gains, running, sems = refs[2 * parts :]
    copies = [
        pltpu.make_async_copy(source, buffer, sems.at[i])
        for i, (source, buffer) in enumerate(zip(sources, buffers))
    ]
    for copy in copies:
        copy.start()
    own_refs, halo_refs = buffers[:parts], buffers[parts:]
    atom_count = own_refs[0].shape[1]
    part_rows = own_refs[0].shape[0] - 3 * basis_count
    own_blocks = atom_count // BLOCK
    halo_blocks = halo_refs[0].shape[1] // BLOCK
    channels, target_total = out.shape
    tile = min(BLOCK, target_total)
    spacing = cutoff / (basis_count - 1)
    root = math.sqrt(math.log2(math.e))
    chan, first_window, own_slot = info[1], info[2], info[3]
    step = 16

    for part in range(parts):
        copies[part].wait()
        copies[parts + part].wait()
        for at in range(0, part_rows, LANES):
            rows = [
                own_refs[part][
                    part_rows + i * basis_count : part_rows + (i + 1) * basis_count,
                    at : at + LANES,
                ].astype(jnp.float32)
                for i in range(3)
            ]
            count = min(LANES, part_rows - at)
            turned = (rows[0] + rows[1] + rows[2]).T
            gains[part * part_rows + at : part * part_rows + at + count] = turned[0:count]

        @pl.loop(0, part_rows // step, unroll=2)
        def _(group):
            rows = pl.ds(pl.multiple_of(group * step, step), step)
            into = pl.ds(pl.multiple_of(part * part_rows + group * step, step), step)
            columns = gains[into]
            factors = [
                jnp.broadcast_to(columns[:, m : m + 1], (step, BLOCK)) for m in range(basis_count)
            ]
            blocks = [(own_refs[part], i, own_slot + i) for i in range(own_blocks)]
            blocks += [(halo_refs[part], i, info[5 + i]) for i in range(halo_blocks)]
            for ref, block, slot in blocks:
                value = ref[rows, block * BLOCK : (block + 1) * BLOCK].astype(jnp.float32)
                for m in range(basis_count):
                    scaled[slot, m, into] = (value * factors[m]).astype(jnp.bfloat16)

    first_target = chan * target_total
    tiles = range(target_total // tile)
    target_blocks = [(first_target + i * tile) // BLOCK for i in tiles]
    target_places = []
    for i in tiles:
        running[i] = jnp.zeros((tile, channels), jnp.float32)
        places = own_tile(positions, first_target, i * tile, tile)
        places = jnp.concatenate([places, jnp.zeros((8 - 3, tile), jnp.float32)]).T
        target_places.append(
            [
                jnp.broadcast_to(places[:, axis : axis + 1] * scale, (tile, BLOCK))
                for axis, scale in enumerate((brick_width, cross_width, cross_width))
            ]
        )

    def add_entry(i, entry):
        x_target, y_target, z_target = target_places[i]
        used = entry < counts[target_blocks[i]]
        listed = lists[target_blocks[i], entry]
        shift = listed + (own_blocks - REACH)
        source_ref = near.at[shift // own_blocks]
        first, second, third = read_places(source_ref, lax.rem(shift, own_blocks), own_blocks, 8)
        first = (first + (listed - REACH).astype(jnp.float32)) * (brick_width / own_blocks)
        second, third = second * cross_width, third * cross_width
        dx = jnp.concatenate([first] * (tile // 8)) - x_target
        dy = jnp.concatenate([second] * (tile // 8)) - y_target
        dz = jnp.concatenate([third] * (tile // 8)) - z_target
        squared = dx * dx + dy * dy + dz * dz
        reach = jnp.sqrt(squared) * (root / spacing)
        envelope = jnp.maximum(1.0 - squared * (1.0 / (cutoff * cutoff)), 0.0)
        envelope = envelope * envelope * used.astype(jnp.float32)
        basis = []
        for m in range(basis_count):
            gap = reach - m * root
            basis.append((jnp.exp2(-(gap * gap)) * envelope).astype(jnp.bfloat16))
        source = scaled.at[listed - first_window]
        running[i] += lax.dot_general(
            jnp.concatenate(basis, axis=1),
            jnp.concatenate([source[m] for m in range(basis_count)], axis=1),
            NT,
            preferred_element_type=jnp.float32,
        )

    longest = counts[target_blocks[0]]
    for block in target_blocks[1:]:
        longest = jnp.maximum(longest, counts[block])

    @pl.loop(0, longest)
    def _(entry):
        for i in tiles:
            add_entry(i, entry)

    for i in tiles:
        summed = running[i].T
        for part in range(parts):
            own = own_tile(own_refs[part].at[0:part_rows], first_target, i * tile, tile)
            out[pl.ds(part * part_rows, part_rows), i * tile : (i + 1) * tile] = (
                own.astype(jnp.float32) + summed[part * part_rows : (part + 1) * part_rows]
            )


def own_tile(ref, first, start, width):
    if width % LANES == 0:
        return ref[:, pl.ds(pl.multiple_of(first + start, LANES), width)]
    value = ref[...]
    picked = value[:, 0:width]
    for at in range(width, value.shape[1], width):
        picked = jnp.where(first + start == at, value[:, at : at + width], picked)
    return picked


def message_call(info, lists, counts, near, positions, owns, halos, basis_count):
    parts = len(owns)
    own_rows, atom_count = owns[0].shape
    channels = parts * (own_rows - 3 * basis_count)
    slots = (atom_count + halos[0].shape[1]) // BLOCK
    target_total = atom_count // parts
    tile = min(BLOCK, target_total)
    smem, vmem = pl.BlockSpec(memory_space=pltpu.SMEM), pl.BlockSpec(memory_space=pltpu.VMEM)
    moved = [*owns, *halos]
    scratch = [(value.shape, value.dtype) for value in moved] + [
        ((slots, basis_count, channels, BLOCK), jnp.bfloat16),
        ((channels, basis_count), jnp.float32),
        ((target_total // tile, tile, channels), jnp.float32),
    ]
    out = ((channels, target_total), jnp.float32)
    held = [out, (near.shape, near.dtype), (positions.shape, positions.dtype)]
    return pl.pallas_call(
        functools.partial(message_kernel, parts=parts, basis_count=basis_count),
        out_shape=jax.ShapeDtypeStruct(*out),
        in_specs=[smem] * 3 + [vmem] * 2 + [pl.BlockSpec(memory_space=pltpu.HBM)] * len(moved),
        out_specs=vmem,
        scratch_shapes=[pltpu.VMEM(*entry) for entry in scratch]
        + [pltpu.SemaphoreType.DMA((len(moved),))],
        compiler_params=pltpu.CompilerParams(
            vmem_limit_bytes=bytes_of(*scratch, *held) + SMALL_LIMIT
        ),
        cost_estimate=pl.CostEstimate(
            flops=8 * channels * basis_count * BLOCK * target_total,
            bytes_accessed=channels * target_total * 8,
            transcendentals=0,
        ),
        name="messages",
    )(
        info,
        lists,
        counts,
        near,
        positions,
        *(pltpu.with_memory_space_constraint(value, pltpu.HBM) for value in moved),
    )


def mixing_kernel(info, base, ewald, gain, *refs, parts, pieces, per_device):
    total = 1 + (parts - 1) * pieces
    in_refs, out_refs = refs[:total], refs[total : 2 * total]
    out, mixed, normed, active, gains = refs[2 * total :]
    channels, width = base.shape
    part_rows = channels // parts
    chan, first_piece = info[1], info[4]
    for at in range(0, channels, LANES):
        gains[at : at + LANES] = jnp.broadcast_to(gain[:, at : at + LANES], (8, LANES)).T
    squares = jnp.zeros((1, width), jnp.float32)
    for part in range(parts):
        other = lax.rem(chan + part, parts)
        for start in range(0, part_rows, per_device):
            rows = pl.ds(part * part_rows + start, per_device)
            piece = ewald[(start // per_device) * parts + other].astype(jnp.float32)
            value = (base[rows] + piece).astype(jnp.bfloat16).astype(jnp.float32)
            mixed[rows] = value
            squares = squares + jnp.sum(value * value, axis=0, keepdims=True)
    factor = lax.rsqrt(squares * (1.0 / channels) + epsilon)
    for part in range(parts):
        other = lax.rem(chan + part, parts)
        rows = pl.ds(part * part_rows, part_rows)
        here = pl.ds(pl.multiple_of(other * part_rows, part_rows), part_rows)
        normed[rows] = (mixed[rows] * factor * gains[here, 0:1]).astype(jnp.bfloat16)
    piece_rows = in_refs[0].shape[0] // pieces
    step = min(256, piece_rows)
    for piece in range(pieces):
        at = lax.rem(first_piece + piece, pieces) * piece_rows
        for start in range(0, piece_rows, step):
            rows = pl.ds(pl.multiple_of(at + start, step), step)
            hidden = jnp.dot(
                in_refs[0][rows], normed[0:part_rows], preferred_element_type=jnp.float32
            )
            for part in range(1, parts):
                hidden = hidden + jnp.dot(
                    in_refs[1 + (part - 1) * pieces + piece][start : start + step],
                    normed[part * part_rows : (part + 1) * part_rows],
                    preferred_element_type=jnp.float32,
                )
            bent = hidden * (hidden * hidden * (0.044715 * GELU_SCALE) + GELU_SCALE)
            half = 0.5 * hidden
            active[rows] = (half + half * jnp.tanh(bent)).astype(jnp.bfloat16)
    for part in range(parts):
        count = 1 if part == 0 else pieces
        rows = part_rows // count
        other = lax.rem(chan + part, parts) * part_rows
        for piece in range(count):
            ref = out_refs[part and 1 + (part - 1) * pieces + piece]
            value = jnp.dot(ref[...], active[...], preferred_element_type=jnp.float32)
            at = lax.rem(first_piece + piece, count) * rows
            here = pl.ds(pl.multiple_of(other + at, rows), rows)
            there = pl.ds(pl.multiple_of(part * part_rows + at, rows), rows)
            out[here] = (mixed[there] + value).astype(jnp.bfloat16)


def mixing_call(info, base, ewald, gain, ins, outs, parts, pieces):
    channels, width = base.shape
    hidden = ins[0].shape[0]
    smem = pl.BlockSpec(memory_space=pltpu.SMEM)
    vmem = pl.BlockSpec(memory_space=pltpu.VMEM)
    operands = [base, ewald, gain, *ins, *outs]
    scratch = [
        ((channels, width), jnp.float32),
        ((channels, width), jnp.bfloat16),
        ((hidden, width), jnp.bfloat16),
        ((channels, 8), jnp.float32),
    ]
    held = [((channels, width), jnp.bfloat16), *((v.shape, v.dtype) for v in operands)]
    return pl.pallas_call(
        functools.partial(
            mixing_kernel, parts=parts, pieces=pieces, per_device=ewald.shape[1]
        ),
        out_shape=jax.ShapeDtypeStruct((channels, width), jnp.bfloat16),
        in_specs=[smem] + [vmem] * len(operands),
        out_specs=vmem,
        scratch_shapes=[pltpu.VMEM(*entry) for entry in scratch],
        compiler_params=pltpu.CompilerParams(
            vmem_limit_bytes=bytes_of(*scratch, *held) + SMALL_LIMIT
        ),
        cost_estimate=pl.CostEstimate(
            flops=4 * channels * hidden * width,
            bytes_accessed=4 * channels * hidden,
            transcendentals=hidden * width,
        ),
        name="mixing",
    )(info, *operands)


def chan_parts(value, count):
    return [value] + [
        lax.ppermute(value, "chan", [((i + part) % count, i) for i in range(count)])
        for part in range(1, count)
    ]


def body(
    features, positions, lists, counts, fourier_filter, radial_weights, norm_gain, mlp_in, mlp_out
):
    part_rows, atom_count = features.shape
    bricks, chans = lax.axis_size("brick"), lax.axis_size("chan")
    brick, chan = lax.axis_index("brick"), lax.axis_index("chan")
    blocks_dev = atom_count // BLOCK
    basis_count = radial_weights.shape[0]
    per_device = part_rows // bricks
    padded = -(-per_device // 16) * 16
    width = atom_count // chans
    rim = blocks_dev // 2 * BLOCK

    pieces = 2 if bricks % 2 == 0 else 1
    first_piece = lax.rem(brick, pieces)
    halved = chans == 2 and blocks_dev == 2 * REACH
    if halved:
        lower = chan == 0
        own_slot = jnp.where(lower, REACH, 0)
        halo_slots = [jnp.where(lower, i, blocks_dev + i) for i in range(REACH)]
        first_window = jnp.where(lower, 0, REACH)
    else:
        own_slot = rim // BLOCK
        halo_slots = [i for i in range(rim // BLOCK)]
        halo_slots += [rim // BLOCK + blocks_dev + i for i in range(rim // BLOCK)]
        first_window = 0
    numbers = [brick, chan, first_window, own_slot, first_piece, *halo_slots]
    info = jnp.stack([jnp.asarray(v, jnp.int32) for v in numbers])

    if halved and per_device % 16 == 0:
        sent = pack_call(features, positions, bricks)
        own, first, second = border_call(features, radial_weights, rim)
    else:
        sent = features.reshape(bricks, per_device, atom_count)
        sent = to_groups(jnp.pad(sent, ((0, 0), (0, padded - per_device), (0, 0))))
        place_rows = split_places(positions, blocks_dev)[None]
        place_rows = jnp.broadcast_to(place_rows, (bricks, *place_rows.shape[1:]))
        sent = jnp.concatenate([sent, place_rows], axis=1)
        rest, radial = radial_weights, []
        for _ in range(3):
            radial.append(lax.reduce_precision(rest, 8, 7))
            rest = rest - radial[-1]
        radial = jnp.concatenate(radial).astype(jnp.bfloat16)
        radial = jnp.pad(radial, ((0, 0), (0, atom_count - part_rows)))
        own = jnp.concatenate([features, radial])
        first, second = features[:, atom_count - rim :], features[:, :rim]
        if halved:
            first, second = jnp.where(lower, first, second), jnp.where(lower, second, first)
    gathered = lax.all_to_all(sent, "brick", 0, 0)

    owns = chan_parts(own, chans)
    if halved:
        names = ("brick", "chan")

        def source(low_from, high_from):
            pairs = []
            for i in range(bricks):
                pairs.append((((i - 1) % bricks) * 2 + low_from, i * 2))
                pairs.append((((i + 1) % bricks) * 2 + high_from, i * 2 + 1))
            return pairs

        halos = [
            lax.ppermute(first, names, source(0, 1)),
            lax.ppermute(second, names, source(1, 0)),
        ]
    else:
        before = lax.ppermute(first, "brick", [(i, (i + 1) % bricks) for i in range(bricks)])
        after = lax.ppermute(second, "brick", [((i + 1) % bricks, i) for i in range(bricks)])
        halos = chan_parts(jnp.concatenate([before, after], axis=1), chans)

    if padded == per_device:
        filters, fetched_in, fetched_out = pick_call(
            info, (fourier_filter, mlp_in, mlp_out), (bricks, pieces, pieces)
        )
    else:
        filters = lax.dynamic_slice_in_dim(fourier_filter, brick * per_device, per_device, 0)
        filters = jnp.pad(filters, ((0, padded - per_device), (0, 0)))
        fetched_in, fetched_out = (
            lax.dynamic_slice_in_dim(
                value, first_piece * (value.shape[0] // pieces), value.shape[0] // pieces, 0
            )
            for value in (mlp_in, mlp_out)
        )
    ins = [mlp_in, *chan_parts(fetched_in, chans)[1:]]
    outs = [mlp_out, *chan_parts(fetched_out, chans)[1:]]

    halves = chans if width % BLOCK == 0 else 1
    ewald, near = ewald_call(info, gathered, filters, halves)
    ewald = ewald[:, :per_device]
    if halves != chans:
        ewald = ewald.reshape(bricks, per_device, chans, width)
        ewald = ewald.transpose(0, 2, 1, 3).reshape(bricks * chans, per_device, width)
    arrived = lax.all_to_all(ewald, ("brick", "chan"), 0, 0)

    ins = swap_pieces(ins, bricks, pieces)
    outs = swap_pieces(outs, bricks, pieces)
    base = message_call(
        info, lists, counts, near, positions, owns, halos, basis_count
    )
    return mixing_call(info, base, arrived, norm_gain[None, :], ins, outs, chans, pieces)


def swap_pieces(values, bricks, pieces):
    if pieces == 1:
        return values
    swapped = [values[0]]
    for value in values[1:]:
        swapped += [value, lax.ppermute(value, "brick", [(i, i ^ 1) for i in range(bricks)])]
    return swapped


def solution(mesh):
    placed = (
        P("chan", "brick"),
        P(None, "brick"),
        P("brick", None),
        P("brick"),
        P("chan", None),
        P(None, "chan"),
        P(),
        P(None, "chan"),
        P("chan", None),
    )

    return jax.shard_map(
        body, mesh=mesh, in_specs=placed, out_specs=P(None, ("brick", "chan")), check_vma=False
    )
```

```python
import functools
import math

import jax
import jax.numpy as jnp
from jax import lax
from jax.experimental import pallas as pl
from jax.experimental.pallas import tpu as pltpu
from jax.sharding import PartitionSpec as P


KSIDE = 16
BLOCK = 128
REACH = 2
brick_width = 4.0
cross_width = 8.0
cutoff = 2.0
epsilon = 1e-06

HALF = KSIDE // 2
PLANE = KSIDE * KSIDE
GELU_SCALE = math.sqrt(2.0 / math.pi)
PIECES = 2
PLACE_ROWS = 3 * PIECES
LANES = 128
SMALL_LIMIT = 4 * 1024 * 1024
NT = (((1,), (1,)), ((), ()))

SIN_TERMS = (3.14159258, -5.1677069, 2.55003164, -0.59804645, 0.07722225)
COS_TERMS = (0.99999995, -4.93479286, 4.05841191, -1.33188016, 0.2196968)


def horner(terms, squared):
    value = squared * terms[-1] + terms[-2]
    for term in terms[-3::-1]:
        value = value * squared + term
    return value


def turn_cos_sin(turns):
    near = turns - jnp.round(turns)
    squared = near * near
    sine = near * horner(SIN_TERMS, squared)
    double = sine + sine
    return 1.0 - double * sine, double * horner(COS_TERMS, squared)


def same_row(ref, row, count):
    return ref[pl.ds(row, count, stride=0), :]


def read_places(ref, group, groups, count):
    values = []
    for axis in range(3):
        pieces = [
            same_row(ref, (piece * 3 + axis) * groups + group, count) for piece in range(PIECES)
        ]
        values.append(sum(pieces[1:], pieces[0]))
    return values


def to_groups(value):
    groups = value.shape[-1] // LANES
    value = value.reshape(*value.shape[:-1], groups, LANES)
    value = jnp.swapaxes(value, -2, -3)
    return value.reshape(*value.shape[:-3], -1, LANES)


def split_places(positions, blocks_dev):
    atom_count = positions.shape[1]
    own_block = (jnp.arange(atom_count, dtype=jnp.int32) // BLOCK).astype(jnp.float32)
    rest = jnp.stack([positions[0] * blocks_dev - own_block, positions[1], positions[2]])
    pieces = []
    for _ in range(PIECES):
        pieces.append(lax.reduce_precision(rest, 8, 7))
        rest = rest - pieces[-1]
    return jnp.concatenate(pieces).astype(jnp.bfloat16).reshape(-1, LANES)


def three_pieces(value):
    high = value.astype(jnp.bfloat16).astype(jnp.float32)
    value = value - high
    middle = value.astype(jnp.bfloat16).astype(jnp.float32)
    return high, middle, value - middle


def pack_kernel(features, positions, sent, places, whole, rows, sems):
    bricks, _, _ = sent.shape
    part_rows, atom_count = features.shape
    per_device = part_rows // bricks
    groups = atom_count // LANES
    copies = [
        pltpu.make_async_copy(positions, places, sems.at[0]),
        pltpu.make_async_copy(features, whole, sems.at[1]),
    ]
    for copy in copies:
        copy.start()
    blocks_dev = atom_count // BLOCK
    own_block = lax.broadcasted_iota(jnp.int32, (1, atom_count), 1) // BLOCK
    copies[0].wait()
    places[0:1] = places[0:1] * blocks_dev - own_block.astype(jnp.float32)
    rest = places[...]
    for piece in range(PIECES):
        high = rest.astype(jnp.bfloat16).astype(jnp.float32)
        rest = rest - high
        for axis in range(3):
            for group in range(groups):
                at = (piece * 3 + axis) * groups + group
                rows[at : at + 1] = high[axis : axis + 1, group * LANES : (group + 1) * LANES]
    place_rows = rows[...].astype(jnp.bfloat16)
    copies[1].wait()
    for device in range(bricks):
        here = slice(device * per_device, (device + 1) * per_device)
        for group in range(groups):
            sent[device, group * per_device : (group + 1) * per_device] = whole[
                here, group * LANES : (group + 1) * LANES
            ]
        sent[device, groups * per_device :] = place_rows


def pack_call(features, positions, bricks):
    part_rows, atom_count = features.shape
    rows = (part_rows // bricks + PLACE_ROWS) * (atom_count // LANES)
    return pl.pallas_call(
        pack_kernel,
        out_shape=jax.ShapeDtypeStruct((bricks, rows, LANES), jnp.bfloat16),
        in_specs=[pl.BlockSpec(memory_space=pltpu.HBM)] * 2,
        out_specs=pl.BlockSpec(memory_space=pltpu.VMEM),
        scratch_shapes=[
            pltpu.VMEM(positions.shape, positions.dtype),
            pltpu.VMEM(features.shape, features.dtype),
            pltpu.VMEM((PLACE_ROWS * (atom_count // LANES), LANES), jnp.float32),
            pltpu.SemaphoreType.DMA((2,)),
        ],
        compiler_params=pltpu.CompilerParams(vmem_limit_bytes=SMALL_LIMIT),
        name="pack",
    )(*(pltpu.with_memory_space_constraint(v, pltpu.HBM) for v in (features, positions)))


def border_kernel(features, radial, own, first, second, whole, gains, sems):
    part_rows, atom_count = features.shape
    basis_count = radial.shape[0]
    rim = first.shape[1]
    copies = [
        pltpu.make_async_copy(radial, gains, sems.at[0]),
        pltpu.make_async_copy(features, whole, sems.at[1]),
    ]
    for copy in copies:
        copy.start()
    copies[0].wait()
    own[part_rows:] = jnp.zeros((3 * basis_count, atom_count), jnp.bfloat16)
    for i, piece in enumerate(three_pieces(gains[...])):
        at = part_rows + i * basis_count
        own[at : at + basis_count, 0:part_rows] = piece.astype(jnp.bfloat16)
    copies[1].wait()
    own[0:part_rows] = whole[...]
    lower = lax.axis_index("chan") == 0

    @pl.when(lower)
    def _():
        first[...] = whole[:, atom_count - rim :]
        second[...] = whole[:, 0:rim]

    @pl.when(jnp.logical_not(lower))
    def _():
        first[...] = whole[:, 0:rim]
        second[...] = whole[:, atom_count - rim :]


def border_call(features, radial, rim):
    part_rows, atom_count = features.shape
    vmem = pl.BlockSpec(memory_space=pltpu.VMEM)
    outs = [(part_rows + 3 * radial.shape[0], atom_count), (part_rows, rim), (part_rows, rim)]
    return pl.pallas_call(
        border_kernel,
        out_shape=[jax.ShapeDtypeStruct(shape, jnp.bfloat16) for shape in outs],
        in_specs=[pl.BlockSpec(memory_space=pltpu.HBM)] * 2,
        out_specs=[vmem] * 3,
        scratch_shapes=[
            pltpu.VMEM(features.shape, features.dtype),
            pltpu.VMEM(radial.shape, radial.dtype),
            pltpu.SemaphoreType.DMA((2,)),
        ],
        compiler_params=pltpu.CompilerParams(vmem_limit_bytes=SMALL_LIMIT),
        name="border",
    )(*(pltpu.with_memory_space_constraint(v, pltpu.HBM) for v in (features, radial)))


def pick_kernel(info, *refs):
    count = len(refs) // 2
    sources, targets, sems = refs[:count], refs[count:-1], refs[-1]
    copies = []
    for i, (source, target) in enumerate(zip(sources, targets)):
        rows = target.shape[0]
        index = info[0] if i == 0 else info[4]
        here = pl.ds(pl.multiple_of(index * rows, rows), rows)
        copies.append(pltpu.make_async_copy(source.at[here], target, sems.at[i]))
        copies[i].start()
    for copy in copies:
        copy.wait()


def pick_call(info, values, counts):
    smem, vmem = pl.BlockSpec(memory_space=pltpu.SMEM), pl.BlockSpec(memory_space=pltpu.VMEM)
    return pl.pallas_call(
        pick_kernel,
        out_shape=[
            jax.ShapeDtypeStruct((v.shape[0] // count, v.shape[1]), v.dtype)
            for v, count in zip(values, counts)
        ],
        in_specs=[smem] + [pl.BlockSpec(memory_space=pltpu.HBM)] * len(values),
        out_specs=[vmem] * len(values),
        scratch_shapes=[pltpu.SemaphoreType.DMA((len(values),))],
        compiler_params=pltpu.CompilerParams(vmem_limit_bytes=SMALL_LIMIT),
        name="pick",
    )(info, *(pltpu.with_memory_space_constraint(v, pltpu.HBM) for v in values))


def ewald_kernel(
    info,
    gathered,
    filters,
    out,
    near,
    places,
    steps,
    table,
    depth_table,
    scaled,
    sums,
    weights,
    *,
    halves,
):
    bricks, channels, atom_count = out.shape[0] // halves, out.shape[1], out.shape[2] * halves
    groups = atom_count // LANES
    total = bricks * atom_count
    blocks_dev = atom_count // BLOCK
    inverse = 1.0 / math.sqrt(total)
    row = lax.broadcasted_iota(jnp.int32, (HALF, 1), 0)
    wave = row.astype(jnp.float32) + 1.0
    quarter = HALF // 2
    upper_rows = row >= quarter
    mid_wave = lax.rem(row, quarter).astype(jnp.float32) + 0.5

    def depth_row(ref, k, sine):
        at = (k // quarter) * 4 * quarter + sine * 2 * quarter + quarter + k % quarter
        return same_row(ref, at, channels)

    def make_tables(brick, slot):
        places[slot] = gathered[brick, channels * groups :].astype(jnp.float32)
        alongs = []
        for group in range(groups):
            first, second, third = read_places(places.at[slot], group, groups, HALF)
            start = brick * blocks_dev + group * LANES // BLOCK
            along = (first + start.astype(jnp.float32)) * (1.0 / (blocks_dev * bricks))
            alongs.append((along, second, third))
            for i, turns in enumerate((HALF * along, quarter * second, quarter * third)):
                at = i * groups + group
                steps[slot, 0, at : at + 1] = turns[0:1]
        steps[slot, 0], steps[slot, 1] = turn_cos_sin(steps[slot, 0])
        step_cos, step_sin = steps.at[slot, 0], steps.at[slot, 1]
        for group in range(groups):
            along, second, third = alongs[group]
            here = brick * groups + group
            rows = depth_table.at[here]
            low_cos, low_sin = turn_cos_sin(mid_wave * jnp.where(upper_rows, third, second))
            by_cos, by_sin = (
                jnp.where(
                    upper_rows,
                    same_row(ref, 2 * groups + group, HALF),
                    same_row(ref, groups + group, HALF),
                )
                for ref in (step_cos, step_sin)
            )
            rows[0:HALF], rows[HALF : 2 * HALF] = low_cos, low_sin
            rows[2 * HALF : 3 * HALF] = low_cos * by_cos - low_sin * by_sin
            rows[3 * HALF :] = low_cos * by_sin + low_sin * by_cos

            low_cos, low_sin = turn_cos_sin(wave * along - 0.5 * (second + third))
            by_cos, by_sin = same_row(step_cos, group, HALF), same_row(step_sin, group, HALF)
            x_cos = jnp.concatenate([low_cos, low_cos * by_cos - low_sin * by_sin], axis=0)
            x_sin = jnp.concatenate([low_sin, low_cos * by_sin + low_sin * by_cos], axis=0)
            for k in range(HALF):
                at = (k // quarter) * 2 * HALF + k % quarter
                cos_row, sin_row = same_row(rows, at, KSIDE), same_row(rows, at + HALF, KSIDE)
                a, b = x_cos * cos_row, x_sin * sin_row
                c, d = x_sin * cos_row, x_cos * sin_row
                above, below = (HALF + k) * KSIDE, (HALF - 1 - k) * KSIDE
                table[here, above : above + KSIDE] = (a - b).astype(jnp.bfloat16)
                table[here, PLANE + above : PLANE + above + KSIDE] = (c + d).astype(jnp.bfloat16)
                table[here, below : below + KSIDE] = (a + b).astype(jnp.bfloat16)
                table[here, PLANE + below : PLANE + below + KSIDE] = (c - d).astype(jnp.bfloat16)
            values = gathered[brick, group * channels : (group + 1) * channels].astype(jnp.float32)
            for k in range(KSIDE):
                factor = depth_row(rows, k % HALF, k // HALF)
                scaled[slot, group, k * channels : (k + 1) * channels] = (values * factor).astype(
                    jnp.bfloat16
                )

    def table_of(brick):
        return jnp.concatenate([table[brick * groups + group] for group in range(groups)], axis=1)

    def add_sums(brick, slot):
        rows = jnp.concatenate([scaled[slot, group] for group in range(groups)], axis=1)
        sums[...] += lax.dot_general(rows, table_of(brick), NT, preferred_element_type=jnp.float32)

    sums[...] = jnp.zeros_like(sums)
    for step in range(3):
        neighbour = lax.rem(info[0] + (step - 1 + bricks), bricks)
        near[step] = gathered[neighbour, channels * groups :].astype(jnp.float32)

    turn = 8
    turns = (bricks - 1) // turn
    make_tables(jnp.int32(0), 0)

    @pl.loop(0, turns)
    def _(at):
        for step in range(turn):
            add_sums(turn * at + step, step % 2)
            make_tables(turn * at + step + 1, (step + 1) % 2)

    for brick in range(turn * turns, bricks):
        add_sums(brick, brick % 2)
        if brick + 1 < bricks:
            make_tables(jnp.int32(brick + 1), (brick + 1) % 2)

    for k in range(HALF):
        upper = filters[:, pl.ds((HALF + k) * PLANE, PLANE)]
        lower = filters[:, pl.ds((HALF - 1 - k) * PLANE, PLANE)]
        both, apart = (upper + lower) * inverse, (upper - lower) * inverse
        cos_rows = pl.ds(k * channels, channels)
        sin_rows = pl.ds((HALF + k) * channels, channels)
        cos_real, cos_imag = sums[cos_rows, 0:PLANE], sums[cos_rows, PLANE:]
        sin_real, sin_imag = sums[sin_rows, 0:PLANE], sums[sin_rows, PLANE:]
        for row_part, first_part, value in (
            (cos_rows, 0, both * cos_real - apart * sin_imag),
            (cos_rows, PLANE, both * cos_imag + apart * sin_real),
            (sin_rows, 0, apart * cos_imag + both * sin_real),
            (sin_rows, PLANE, both * sin_imag - apart * cos_real),
        ):
            value = value.astype(jnp.bfloat16)
            for at in range(0, PLANE, LANES):
                weights[(first_part + at) // LANES, row_part] = value[:, at : at + LANES]

    @pl.loop(0, bricks, unroll=16)
    def _(brick):
        coefficients = jnp.concatenate(
            [weights[at] for at in range(2 * PLANE // LANES)], axis=1
        )
        mixed = jnp.dot(coefficients, table_of(brick), preferred_element_type=jnp.float32)
        values = []
        for group in range(groups):
            rows = depth_table.at[brick * groups + group]
            lanes = slice(group * LANES, (group + 1) * LANES)
            value = mixed[0:channels, lanes] * depth_row(rows, 0, 0)
            for k in range(1, KSIDE):
                part = mixed[k * channels : (k + 1) * channels, lanes]
                value = value + part * depth_row(rows, k % HALF, k // HALF)
            values.append(value)
        value = jnp.concatenate(values, axis=1)
        value = (value * inverse).astype(jnp.bfloat16)
        width = atom_count // halves
        for part in range(halves):
            out[brick * halves + part] = value[:, part * width : (part + 1) * width]


def bytes_of(*shapes):
    total = 0
    for shape, dtype in shapes:
        padded = [*shape[:-2], -(-shape[-2] // 16) * 16, -(-shape[-1] // LANES) * LANES]
        total += math.prod(padded) * jnp.dtype(dtype).itemsize
    return total


def ewald_call(info, gathered, filters, halves):
    bricks, channels = gathered.shape[0], filters.shape[0]
    groups = gathered.shape[1] // (channels + PLACE_ROWS)
    atom_count = groups * LANES
    total = bricks * atom_count
    rows = KSIDE * channels
    scratch = [
        ((2, PLACE_ROWS * groups, LANES), jnp.float32),
        ((2, 2, 3 * groups, LANES), jnp.float32),
        ((total // LANES, 2 * PLANE, LANES), jnp.bfloat16),
        ((total // LANES, 2 * KSIDE, LANES), jnp.float32),
        ((2, atom_count // LANES, rows, LANES), jnp.bfloat16),
        ((rows, 2 * PLANE), jnp.float32),
        ((2 * PLANE // LANES, rows, LANES), jnp.bfloat16),
    ]
    out = ((bricks * halves, channels, atom_count // halves), jnp.bfloat16)
    near = ((3, PLACE_ROWS * groups, LANES), jnp.float32)
    held = [out, near, (gathered.shape, gathered.dtype), (filters.shape, filters.dtype)]
    smem, vmem = pl.BlockSpec(memory_space=pltpu.SMEM), pl.BlockSpec(memory_space=pltpu.VMEM)
    return pl.pallas_call(
        functools.partial(ewald_kernel, halves=halves),
        out_shape=(jax.ShapeDtypeStruct(*out), jax.ShapeDtypeStruct(*near)),
        in_specs=[smem, vmem, vmem],
        out_specs=(vmem, vmem),
        scratch_shapes=[pltpu.VMEM(*entry) for entry in scratch],
        compiler_params=pltpu.CompilerParams(
            vmem_limit_bytes=bytes_of(*scratch, *held) + SMALL_LIMIT
        ),
        cost_estimate=pl.CostEstimate(
            flops=8 * rows * PLANE * total,
            bytes_accessed=gathered.size * 2 + filters.size * 4,
            transcendentals=0,
        ),
        name="ewald",
    )(info, gathered, filters)


def message_kernel(info, lists, counts, near, positions, *refs, parts, basis_count):
    sources = refs[: 2 * parts]
    out, *buffers, scaled, gains, running, sems = refs[2 * parts :]
    copies = [
        pltpu.make_async_copy(source, buffer, sems.at[i])
        for i, (source, buffer) in enumerate(zip(sources, buffers))
    ]
    for copy in copies:
        copy.start()
    own_refs, halo_refs = buffers[:parts], buffers[parts:]
    atom_count = own_refs[0].shape[1]
    part_rows = own_refs[0].shape[0] - 3 * basis_count
    own_blocks = atom_count // BLOCK
    halo_blocks = halo_refs[0].shape[1] // BLOCK
    channels, target_total = out.shape
    tile = min(BLOCK, target_total)
    spacing = cutoff / (basis_count - 1)
    root = math.sqrt(math.log2(math.e))
    chan, first_window, own_slot = info[1], info[2], info[3]
    step = 16

    for part in range(parts):
        copies[part].wait()
        copies[parts + part].wait()
        for at in range(0, part_rows, LANES):
            rows = [
                own_refs[part][
                    part_rows + i * basis_count : part_rows + (i + 1) * basis_count,
                    at : at + LANES,
                ].astype(jnp.float32)
                for i in range(3)
            ]
            count = min(LANES, part_rows - at)
            turned = (rows[0] + rows[1] + rows[2]).T
            gains[part * part_rows + at : part * part_rows + at + count] = turned[0:count]

        @pl.loop(0, part_rows // step, unroll=2)
        def _(group):
            rows = pl.ds(pl.multiple_of(group * step, step), step)
            into = pl.ds(pl.multiple_of(part * part_rows + group * step, step), step)
            columns = gains[into]
            factors = [
                jnp.broadcast_to(columns[:, m : m + 1], (step, BLOCK)) for m in range(basis_count)
            ]
            blocks = [(own_refs[part], i, own_slot + i) for i in range(own_blocks)]
            blocks += [(halo_refs[part], i, info[5 + i]) for i in range(halo_blocks)]
            for ref, block, slot in blocks:
                value = ref[rows, block * BLOCK : (block + 1) * BLOCK].astype(jnp.float32)
                for m in range(basis_count):
                    scaled[slot, m, into] = (value * factors[m]).astype(jnp.bfloat16)

    first_target = chan * target_total
    tiles = range(target_total // tile)
    target_blocks = [(first_target + i * tile) // BLOCK for i in tiles]
    target_places = []
    for i in tiles:
        running[i] = jnp.zeros((tile, channels), jnp.float32)
        places = own_tile(positions, first_target, i * tile, tile)
        places = jnp.concatenate([places, jnp.zeros((8 - 3, tile), jnp.float32)]).T
        target_places.append(
            [
                jnp.broadcast_to(places[:, axis : axis + 1] * scale, (tile, BLOCK))
                for axis, scale in enumerate((brick_width, cross_width, cross_width))
            ]
        )

    def add_entry(i, entry):
        x_target, y_target, z_target = target_places[i]
        used = entry < counts[target_blocks[i]]
        listed = lists[target_blocks[i], entry]
        shift = listed + (own_blocks - REACH)
        source_ref = near.at[shift // own_blocks]
        first, second, third = read_places(source_ref, lax.rem(shift, own_blocks), own_blocks, 8)
        first = (first + (listed - REACH).astype(jnp.float32)) * (brick_width / own_blocks)
        second, third = second * cross_width, third * cross_width
        dx = jnp.concatenate([first] * (tile // 8)) - x_target
        dy = jnp.concatenate([second] * (tile // 8)) - y_target
        dz = jnp.concatenate([third] * (tile // 8)) - z_target
        squared = dx * dx + dy * dy + dz * dz
        reach = jnp.sqrt(squared) * (root / spacing)
        envelope = jnp.maximum(1.0 - squared * (1.0 / (cutoff * cutoff)), 0.0)
        envelope = envelope * envelope * used.astype(jnp.float32)
        basis = []
        for m in range(basis_count):
            gap = reach - m * root
            basis.append((jnp.exp2(-(gap * gap)) * envelope).astype(jnp.bfloat16))
        source = scaled.at[listed - first_window]
        running[i] += lax.dot_general(
            jnp.concatenate(basis, axis=1),
            jnp.concatenate([source[m] for m in range(basis_count)], axis=1),
            NT,
            preferred_element_type=jnp.float32,
        )

    longest = counts[target_blocks[0]]
    for block in target_blocks[1:]:
        longest = jnp.maximum(longest, counts[block])

    @pl.loop(0, longest)
    def _(entry):
        for i in tiles:
            add_entry(i, entry)

    for i in tiles:
        summed = running[i].T
        for part in range(parts):
            own = own_tile(own_refs[part].at[0:part_rows], first_target, i * tile, tile)
            out[pl.ds(part * part_rows, part_rows), i * tile : (i + 1) * tile] = (
                own.astype(jnp.float32) + summed[part * part_rows : (part + 1) * part_rows]
            )


def own_tile(ref, first, start, width):
    if width % LANES == 0:
        return ref[:, pl.ds(pl.multiple_of(first + start, LANES), width)]
    value = ref[...]
    picked = value[:, 0:width]
    for at in range(width, value.shape[1], width):
        picked = jnp.where(first + start == at, value[:, at : at + width], picked)
    return picked


def message_call(info, lists, counts, near, positions, owns, halos, basis_count):
    parts = len(owns)
    own_rows, atom_count = owns[0].shape
    channels = parts * (own_rows - 3 * basis_count)
    slots = (atom_count + halos[0].shape[1]) // BLOCK
    target_total = atom_count // parts
    tile = min(BLOCK, target_total)
    smem, vmem = pl.BlockSpec(memory_space=pltpu.SMEM), pl.BlockSpec(memory_space=pltpu.VMEM)
    moved = [*owns, *halos]
    scratch = [(value.shape, value.dtype) for value in moved] + [
        ((slots, basis_count, channels, BLOCK), jnp.bfloat16),
        ((channels, basis_count), jnp.float32),
        ((target_total // tile, tile, channels), jnp.float32),
    ]
    out = ((channels, target_total), jnp.float32)
    held = [out, (near.shape, near.dtype), (positions.shape, positions.dtype)]
    return pl.pallas_call(
        functools.partial(message_kernel, parts=parts, basis_count=basis_count),
        out_shape=jax.ShapeDtypeStruct(*out),
        in_specs=[smem] * 3 + [vmem] * 2 + [pl.BlockSpec(memory_space=pltpu.HBM)] * len(moved),
        out_specs=vmem,
        scratch_shapes=[pltpu.VMEM(*entry) for entry in scratch]
        + [pltpu.SemaphoreType.DMA((len(moved),))],
        compiler_params=pltpu.CompilerParams(
            vmem_limit_bytes=bytes_of(*scratch, *held) + SMALL_LIMIT
        ),
        cost_estimate=pl.CostEstimate(
            flops=8 * channels * basis_count * BLOCK * target_total,
            bytes_accessed=channels * target_total * 8,
            transcendentals=0,
        ),
        name="messages",
    )(
        info,
        lists,
        counts,
        near,
        positions,
        *(pltpu.with_memory_space_constraint(value, pltpu.HBM) for value in moved),
    )


def mixing_kernel(info, base, ewald, gain, *refs, parts, pieces, per_device):
    total = 1 + (parts - 1) * pieces
    in_refs, out_refs = refs[:total], refs[total : 2 * total]
    out, mixed, normed, active, gains, results, sems = refs[2 * total :]
    channels, width = base.shape
    part_rows = channels // parts
    chan, first_piece = info[1], info[4]
    for at in range(0, channels, LANES):
        gains[at : at + LANES] = jnp.broadcast_to(gain[:, at : at + LANES], (8, LANES)).T
    squares = jnp.zeros((1, width), jnp.float32)
    for part in range(parts):
        other = lax.rem(chan + part, parts)
        for start in range(0, part_rows, per_device):
            rows = pl.ds(part * part_rows + start, per_device)
            piece = ewald[(start // per_device) * parts + other].astype(jnp.float32)
            value = (base[rows] + piece).astype(jnp.bfloat16).astype(jnp.float32)
            mixed[rows] = value
            squares = squares + jnp.sum(value * value, axis=0, keepdims=True)
    factor = lax.rsqrt(squares * (1.0 / channels) + epsilon)
    for part in range(parts):
        other = lax.rem(chan + part, parts)
        rows = pl.ds(part * part_rows, part_rows)
        here = pl.ds(pl.multiple_of(other * part_rows, part_rows), part_rows)
        normed[rows] = (mixed[rows] * factor * gains[here, 0:1]).astype(jnp.bfloat16)
    piece_rows = in_refs[0].shape[0] // pieces
    step = min(256, piece_rows)
    for piece in range(pieces):
        at = lax.rem(first_piece + piece, pieces) * piece_rows
        for start in range(0, piece_rows, step):
            rows = pl.ds(pl.multiple_of(at + start, step), step)
            hidden = jnp.dot(
                in_refs[0][rows], normed[0:part_rows], preferred_element_type=jnp.float32
            )
            for part in range(1, parts):
                hidden = hidden + jnp.dot(
                    in_refs[1 + (part - 1) * pieces + piece][start : start + step],
                    normed[part * part_rows : (part + 1) * part_rows],
                    preferred_element_type=jnp.float32,
                )
            bent = hidden * (hidden * hidden * (0.044715 * GELU_SCALE) + GELU_SCALE)
            half = 0.5 * hidden
            active[rows] = (half + half * jnp.tanh(bent)).astype(jnp.bfloat16)
    copies = []
    for part in range(parts):
        count = pieces
        rows = part_rows // count
        other = lax.rem(chan + part, parts) * part_rows
        for piece in range(count):
            at = lax.rem(first_piece + piece, count) * rows
            if part == 0:
                weights = out_refs[0][pl.ds(pl.multiple_of(at, rows), rows)]
            else:
                weights = out_refs[1 + (part - 1) * pieces + piece][...]
            value = jnp.dot(weights, active[...], preferred_element_type=jnp.float32)
            here = pl.ds(pl.multiple_of(other + at, rows), rows)
            there = pl.ds(pl.multiple_of(part * part_rows + at, rows), rows)
            results[there] = (mixed[there] + value).astype(jnp.bfloat16)
            copy = pltpu.make_async_copy(
                results.at[there], out.at[here], sems.at[part * pieces + piece]
            )
            copy.start()
            copies.append(copy)
    for copy in copies:
        copy.wait()


def mixing_call(info, base, ewald, gain, ins, outs, parts, pieces):
    channels, width = base.shape
    hidden = ins[0].shape[0]
    smem = pl.BlockSpec(memory_space=pltpu.SMEM)
    vmem = pl.BlockSpec(memory_space=pltpu.VMEM)
    operands = [base, ewald, gain, *ins, *outs]
    scratch = [
        ((channels, width), jnp.float32),
        ((channels, width), jnp.bfloat16),
        ((hidden, width), jnp.bfloat16),
        ((channels, 8), jnp.float32),
        ((channels, width), jnp.bfloat16),
    ]
    held = [((channels, width), jnp.bfloat16), *((v.shape, v.dtype) for v in operands)]
    return pl.pallas_call(
        functools.partial(
            mixing_kernel, parts=parts, pieces=pieces, per_device=ewald.shape[1]
        ),
        out_shape=jax.ShapeDtypeStruct((channels, width), jnp.bfloat16),
        in_specs=[smem] + [vmem] * len(operands),
        out_specs=pl.BlockSpec(memory_space=pltpu.HBM),
        scratch_shapes=[pltpu.VMEM(*entry) for entry in scratch]
        + [pltpu.SemaphoreType.DMA((parts * pieces,))],
        compiler_params=pltpu.CompilerParams(
            vmem_limit_bytes=bytes_of(*scratch, *held) + SMALL_LIMIT
        ),
        cost_estimate=pl.CostEstimate(
            flops=4 * channels * hidden * width,
            bytes_accessed=4 * channels * hidden,
            transcendentals=hidden * width,
        ),
        name="mixing",
    )(info, *operands)


def chan_parts(value, count):
    return [value] + [
        lax.ppermute(value, "chan", [((i + part) % count, i) for i in range(count)])
        for part in range(1, count)
    ]


def body(
    features, positions, lists, counts, fourier_filter, radial_weights, norm_gain, mlp_in, mlp_out
):
    part_rows, atom_count = features.shape
    bricks, chans = lax.axis_size("brick"), lax.axis_size("chan")
    brick, chan = lax.axis_index("brick"), lax.axis_index("chan")
    blocks_dev = atom_count // BLOCK
    basis_count = radial_weights.shape[0]
    per_device = part_rows // bricks
    padded = -(-per_device // 16) * 16
    width = atom_count // chans
    rim = blocks_dev // 2 * BLOCK

    pieces = 2 if bricks % 2 == 0 else 1
    first_piece = lax.rem(brick, pieces)
    halved = chans == 2 and blocks_dev == 2 * REACH
    if halved:
        lower = chan == 0
        own_slot = jnp.where(lower, REACH, 0)
        halo_slots = [jnp.where(lower, i, blocks_dev + i) for i in range(REACH)]
        first_window = jnp.where(lower, 0, REACH)
    else:
        own_slot = rim // BLOCK
        halo_slots = [i for i in range(rim // BLOCK)]
        halo_slots += [rim // BLOCK + blocks_dev + i for i in range(rim // BLOCK)]
        first_window = 0
    numbers = [brick, chan, first_window, own_slot, first_piece, *halo_slots]
    info = jnp.stack([jnp.asarray(v, jnp.int32) for v in numbers])

    if halved and per_device % 16 == 0:
        sent = pack_call(features, positions, bricks)
        own, first, second = border_call(features, radial_weights, rim)
    else:
        sent = features.reshape(bricks, per_device, atom_count)
        sent = to_groups(jnp.pad(sent, ((0, 0), (0, padded - per_device), (0, 0))))
        place_rows = split_places(positions, blocks_dev)[None]
        place_rows = jnp.broadcast_to(place_rows, (bricks, *place_rows.shape[1:]))
        sent = jnp.concatenate([sent, place_rows], axis=1)
        rest, radial = radial_weights, []
        for _ in range(3):
            radial.append(lax.reduce_precision(rest, 8, 7))
            rest = rest - radial[-1]
        radial = jnp.concatenate(radial).astype(jnp.bfloat16)
        radial = jnp.pad(radial, ((0, 0), (0, atom_count - part_rows)))
        own = jnp.concatenate([features, radial])
        first, second = features[:, atom_count - rim :], features[:, :rim]
        if halved:
            first, second = jnp.where(lower, first, second), jnp.where(lower, second, first)
    gathered = lax.all_to_all(sent, "brick", 0, 0)

    owns = chan_parts(own, chans)
    if halved:
        names = ("brick", "chan")

        def source(low_from, high_from):
            pairs = []
            for i in range(bricks):
                pairs.append((((i - 1) % bricks) * 2 + low_from, i * 2))
                pairs.append((((i + 1) % bricks) * 2 + high_from, i * 2 + 1))
            return pairs

        halos = [
            lax.ppermute(first, names, source(0, 1)),
            lax.ppermute(second, names, source(1, 0)),
        ]
    else:
        before = lax.ppermute(first, "brick", [(i, (i + 1) % bricks) for i in range(bricks)])
        after = lax.ppermute(second, "brick", [((i + 1) % bricks, i) for i in range(bricks)])
        halos = chan_parts(jnp.concatenate([before, after], axis=1), chans)

    if padded == per_device:
        filters, fetched_in, fetched_out = pick_call(
            info, (fourier_filter, mlp_in, mlp_out), (bricks, pieces, pieces)
        )
    else:
        filters = lax.dynamic_slice_in_dim(fourier_filter, brick * per_device, per_device, 0)
        filters = jnp.pad(filters, ((0, padded - per_device), (0, 0)))
        fetched_in, fetched_out = (
            lax.dynamic_slice_in_dim(
                value, first_piece * (value.shape[0] // pieces), value.shape[0] // pieces, 0
            )
            for value in (mlp_in, mlp_out)
        )
    ins = [mlp_in, *chan_parts(fetched_in, chans)[1:]]
    outs = [mlp_out, *chan_parts(fetched_out, chans)[1:]]

    halves = chans if width % BLOCK == 0 else 1
    ewald, near = ewald_call(info, gathered, filters, halves)
    ewald = ewald[:, :per_device]
    if halves != chans:
        ewald = ewald.reshape(bricks, per_device, chans, width)
        ewald = ewald.transpose(0, 2, 1, 3).reshape(bricks * chans, per_device, width)
    arrived = lax.all_to_all(ewald, ("brick", "chan"), 0, 0)

    ins = swap_pieces(ins, bricks, pieces)
    outs = swap_pieces(outs, bricks, pieces)
    base = message_call(
        info, lists, counts, near, positions, owns, halos, basis_count
    )
    return mixing_call(info, base, arrived, norm_gain[None, :], ins, outs, chans, pieces)


def swap_pieces(values, bricks, pieces):
    if pieces == 1:
        return values
    swapped = [values[0]]
    for value in values[1:]:
        swapped += [value, lax.ppermute(value, "brick", [(i, i ^ 1) for i in range(bricks)])]
    return swapped


def solution(mesh):
    placed = (
        P("chan", "brick"),
        P(None, "brick"),
        P("brick", None),
        P("brick"),
        P("chan", None),
        P(None, "chan"),
        P(),
        P(None, "chan"),
        P("chan", None),
    )

    return jax.shard_map(
        body, mesh=mesh, in_specs=placed, out_specs=P(None, ("brick", "chan")), check_vma=False
    )
```
